32 devices in a mesh: dp: 8 (over z, y), tensor: 4 (over x, core).
Axes of the slice: x: 2, y: 2, z: 4, core: 2. Of those that a mesh axis runs over, the one named last changes fastest.
Arguments:
- tokens: bfloat16 [1024, 2048], P('dp'), may hold values from -6 to 6
- lengths: int32 [8], replicated, may hold values from 96 to 128, as said below
- request_adapter: int32 [8], replicated, may hold values from 0 to 63
- token_experts: int32 [1024, 8], P('dp'), may hold values from 0 to 63, as said below
- router_weight: float32 [1024, 8], P('dp'), may hold values from 0.05 to 1
- gate_weight: bfloat16 [128, 2048, 512], P('dp', None, 'tensor'), may hold values from -0.125 to 0.125
- up_weight: bfloat16 [128, 2048, 512], P('dp', None, 'tensor'), may hold values from -0.125 to 0.125
- down_weight: bfloat16 [128, 2048, 512], P('dp', None, 'tensor'), may hold values from -0.1875 to 0.1875
- adapter_input_maps: bfloat16 [2048, 2048], P('tensor', 'dp'), may hold values from -0.125 to 0.125
- adapter_output_maps: bfloat16 [2048, 2, 512], P('dp', None, 'tensor'), may hold values from -1.5 to 1.5
Outputs:
- moe_output: bfloat16 [1024, 2048], P('dp', 'tensor')
The draws below stay inside these ranges and needn't reach their ends.
Inputs may be any that keep to these rules, and one draw needn't show every extreme that they name: `token_experts`: each row names 8 different experts. Among the rows of one request window, each expert is named by at most 28 rows, and one expert, the same in every window, is named by exactly 28 rows, all of live tokens. `lengths`: some request has all 128 tokens live.
All inputs are finite; a program needn't handle non-finite values.
Results may differ from the reference program's by a relative error of at most 0.0065.
Values may be sent and summed in bfloat16 or wider, within the bound.
No kernel may reach another device: no remote copies, remote signals or barrier semaphores. Data moves between devices by JAX's collectives and lax.ppermute only.
A program may use at most 320 MiB of HBM per device.

```python
import math
import jax
import jax.numpy as jnp
from jax import lax

MODEL_WIDTH = 2048
HIDDEN_UNITS = 1024
EXPERTS = 64
TOPK = 8
ADAPTER_COUNT = 64
ADAPTER_RANK = 16
TOK_DEV = 128
REQUESTS = 8
TOKENS = 1024
CAP = 28


def draw_lengths(key, part):
    first_key, second_key = jax.random.split(key)
    drawn = jax.random.randint(first_key, (REQUESTS,), 3 * TOK_DEV // 4, TOK_DEV + 1)
    filled = jax.random.randint(second_key, (), 0, REQUESTS)
    return jnp.where(jnp.arange(REQUESTS) == filled, TOK_DEV, drawn).astype(jnp.int32)


def draw_token_experts(key, part):
    base_count = TOK_DEV * TOPK // EXPERTS
    spread = CAP - base_count
    hottest = jax.random.randint(jax.random.fold_in(key, 1), (), 0, EXPERTS)
    block_keys = jax.random.split(jax.random.fold_in(key, 2), REQUESTS)

    def one_block(block_key):
        key_order, key_steps, key_offset, key_turn = jax.random.split(block_key, 4)
        order = jax.random.permutation(key_order, EXPERTS)
        leading = order[0]
        order = jnp.where(order == hottest, leading, order)
        order = jnp.where(jnp.arange(EXPERTS) == 0, hottest, order)
        steps = jax.random.randint(key_steps, (EXPERTS // 2,), 0, spread + 1)
        steps = steps.at[0].set(spread)
        counts = base_count + jnp.stack([steps, -steps], axis=1).reshape(EXPERTS)
        run_ends = jnp.cumsum(counts)
        offset = jax.random.randint(key_offset, (), 0, 3 * TOK_DEV // 4 - CAP + 1)
        token_pos = jnp.arange(TOK_DEV)
        route_pos = jnp.arange(TOPK)
        entry = route_pos[None, :] * TOK_DEV + (token_pos[:, None] - offset) % TOK_DEV
        which = jnp.sum((entry[:, :, None] >= run_ends[None, None, :]).astype(jnp.int32), axis=2)
        grid = order[which]
        turn = jax.random.randint(key_turn, (TOK_DEV, 1), 0, TOPK)
        source_pos = (route_pos[None, :] - turn) % TOPK
        return jnp.take_along_axis(grid, source_pos, axis=1)
    return jax.vmap(one_block)(block_keys).reshape(TOKENS, TOPK).astype(jnp.int32)


def plant(values, rng, smallest, high):
    spot = [jax.random.randint(jax.random.fold_in(rng, axis), (), 0, length) for axis, length in enumerate(values.shape)]
    widest = values.shape.index(max(values.shape))
    next_to = spot[:widest] + [(spot[widest] + 1) % values.shape[widest]] + spot[widest + 1:]
    return values.at[tuple(spot)].set(smallest).at[tuple(next_to)].set(high)


def block_scale(key, extent, pieces, smallest, high):
    loudness = 1.0
    for dim, parts in pieces:
        draws = jax.random.uniform(jax.random.fold_in(jax.random.fold_in(key, 6), dim), (parts,), jnp.float32, smallest / len(pieces), high / len(pieces))
        loudness = loudness * jnp.repeat(jnp.exp(draws), extent[dim] // parts).reshape((-1,) + (1,) * (len(extent) - 1 - dim))
    return loudness


def bell_draw(own_key, extent, scale, bound, cuts=(), dtype=jnp.bfloat16):
    values = jax.random.normal(own_key, extent, jnp.float32) * scale
    if len(cuts) > 0:
        values = block_scale(own_key, extent, cuts, -0.22, 0.18) * values
    return jnp.clip(values, min=-bound, max=bound).astype(dtype)


def setup_inputs(seed: int = 0) -> dict:
    splits = jax.random.split(jax.random.key(seed), 11)
    tokens = bell_draw(splits[0], (TOKENS, MODEL_WIDTH), 1.0, 6.0, ((0, 8),))
    lengths = draw_lengths(jax.random.fold_in(splits[10], 71), 0)
    request_adapter = plant(jax.random.randint(splits[2], (REQUESTS,), 0, ADAPTER_COUNT), jax.random.fold_in(splits[2], 1), 0, ADAPTER_COUNT - 1).astype(jnp.int32)
    token_experts = draw_token_experts(jax.random.fold_in(splits[10], 71), 0)
    router_weight = jnp.clip(jnp.exp(math.log(1.0) - 2.9957323 * jax.random.uniform(splits[4], (TOKENS, TOPK), jnp.float32) ** block_scale(splits[4], (TOKENS, TOPK), ((0, 8),), -0.2, 0.2)), 0.05, 1.0)
    gate_weight = bell_draw(splits[5], (2 * EXPERTS, MODEL_WIDTH, HIDDEN_UNITS // 2), MODEL_WIDTH ** -0.5, 0.125, ((0, 8), (2, 4)))
    up_weight = bell_draw(splits[6], (2 * EXPERTS, MODEL_WIDTH, HIDDEN_UNITS // 2), MODEL_WIDTH ** -0.5, 0.125, ((0, 8), (2, 4)))
    down_weight = bell_draw(splits[7], (2 * EXPERTS, MODEL_WIDTH, HIDDEN_UNITS // 2), HIDDEN_UNITS ** -0.5, 0.1875, ((0, 8), (2, 4)))
    adapter_input_maps = bell_draw(splits[8], (MODEL_WIDTH, ADAPTER_COUNT * 2 * ADAPTER_RANK), MODEL_WIDTH ** -0.5, 0.125, ((0, 4), (1, 8)))
    adapter_output_maps = bell_draw(splits[9], (ADAPTER_COUNT * 2 * ADAPTER_RANK, 2, HIDDEN_UNITS // 2), ADAPTER_RANK ** -0.5, 1.5, ((0, 8), (2, 4)))
    return {"tokens": tokens, "lengths": lengths, "request_adapter": request_adapter, "token_experts": token_experts, "router_weight": router_weight, "gate_weight": gate_weight, "up_weight": up_weight, "down_weight": down_weight, "adapter_input_maps": adapter_input_maps, "adapter_output_maps": adapter_output_maps}


def slot_layout(block_ids, block_live):
    entries = TOK_DEV * TOPK
    flat_ids = block_ids.reshape(entries)
    token_of = (jnp.arange(entries) // TOPK).astype(jnp.int32)
    entry_live = block_live[token_of]
    expert_hits = ((flat_ids[:, None] == jnp.arange(EXPERTS).astype(jnp.int32)[None, :]) & entry_live[:, None]).astype(jnp.int32)
    position = (jnp.sum(jnp.cumsum(expert_hits, axis=0) * expert_hits, axis=1) - 1).astype(jnp.int32)
    slot_of = jnp.where(entry_live, flat_ids * CAP + position, EXPERTS * CAP).astype(jnp.int32)
    return slot_of, token_of


def fill_block(slot_of, token_of, weights):
    token_table = jnp.full((EXPERTS * CAP + 1,), TOK_DEV, jnp.int32).at[slot_of].set(token_of)
    weight_table = jnp.zeros((EXPERTS * CAP + 1,), jnp.float32).at[slot_of].set(weights)
    return token_table[:EXPERTS * CAP], weight_table[:EXPERTS * CAP]


def reference(tokens, lengths, request_adapter, token_experts, router_weight, gate_weight, up_weight, down_weight, adapter_input_maps, adapter_output_maps):
    double_rank = 2 * ADAPTER_RANK
    half_units = HIDDEN_UNITS // 2
    x_blocks = tokens.reshape(REQUESTS, TOK_DEV, MODEL_WIDTH)
    live_mask = jnp.arange(TOK_DEV).astype(jnp.int32)[None, :] < lengths[:, None]
    selected_adapter = jnp.take(adapter_input_maps.reshape(MODEL_WIDTH, ADAPTER_COUNT, double_rank), request_adapter, axis=1)
    low_rank = jnp.einsum("rtd,drj->rtj", x_blocks.astype(jnp.float32), selected_adapter.astype(jnp.float32), precision=lax.Precision.HIGHEST).astype(jnp.bfloat16)
    slot_of, token_of = jax.vmap(slot_layout)(token_experts.reshape(REQUESTS, TOK_DEV, TOPK), live_mask)
    token_table, weight_table = jax.vmap(fill_block)(slot_of, token_of, router_weight.reshape(REQUESTS, TOK_DEV * TOPK))
    token_table = token_table.reshape(REQUESTS, EXPERTS, CAP).transpose(1, 0, 2)
    weight_table = weight_table.reshape(REQUESTS, EXPERTS, CAP).transpose(1, 0, 2)
    padded_x = jnp.concatenate([x_blocks, jnp.zeros((REQUESTS, 1, MODEL_WIDTH), jnp.bfloat16)], axis=1)
    padded_z = jnp.concatenate([low_rank, jnp.zeros((REQUESTS, 1, double_rank), jnp.bfloat16)], axis=1)
    complete_output_map = jnp.take(adapter_output_maps.reshape(ADAPTER_COUNT, double_rank, HIDDEN_UNITS), request_adapter, axis=0).astype(jnp.float32)
    request_index = jnp.arange(REQUESTS).astype(jnp.int32)[:, None]

    def expert_step(combined, inputs):
        expert, slot_index, slot_weight = inputs
        slot_rows = padded_x[request_index, slot_index].reshape(REQUESTS * CAP, MODEL_WIDTH)
        rank_rows = padded_z[request_index, slot_index].astype(jnp.float32)
        gate_full = jnp.concatenate([gate_weight[expert], gate_weight[expert + EXPERTS]], axis=1)
        up_full = jnp.concatenate([up_weight[expert], up_weight[expert + EXPERTS]], axis=1)
        gate_term = jnp.dot(slot_rows, gate_full, preferred_element_type=jnp.float32).reshape(REQUESTS, CAP, HIDDEN_UNITS)
        gate_term = gate_term + jnp.einsum("rcj,rjf->rcf", rank_rows[..., :ADAPTER_RANK], complete_output_map[:, :ADAPTER_RANK], precision=lax.Precision.HIGHEST)
        up_term = jnp.dot(slot_rows, up_full, preferred_element_type=jnp.float32).reshape(REQUESTS, CAP, HIDDEN_UNITS)
        up_term = up_term + jnp.einsum("rcj,rjf->rcf", rank_rows[..., ADAPTER_RANK:], complete_output_map[:, ADAPTER_RANK:], precision=lax.Precision.HIGHEST)
        hidden = (jax.nn.silu(gate_term) * up_term).astype(jnp.bfloat16).reshape(REQUESTS * CAP, HIDDEN_UNITS)
        lower_out = jnp.dot(hidden[:, :half_units], down_weight[expert].T, preferred_element_type=jnp.float32).astype(jnp.bfloat16)
        upper_out = jnp.dot(hidden[:, half_units:], down_weight[expert + EXPERTS].T, preferred_element_type=jnp.float32).astype(jnp.bfloat16)
        expert_out = (lower_out.astype(jnp.float32) + upper_out.astype(jnp.float32)) * slot_weight.reshape(REQUESTS * CAP, 1)
        target = (request_index * (TOK_DEV + 1) + slot_index).reshape(REQUESTS * CAP)
        return combined.at[target].add(expert_out), None

    start_sum = jnp.zeros((REQUESTS * (TOK_DEV + 1), MODEL_WIDTH), jnp.float32)
    combined, _unused = lax.scan(expert_step, start_sum, (jnp.arange(EXPERTS).astype(jnp.int32), token_table, weight_table))
    return combined.reshape(REQUESTS, TOK_DEV + 1, MODEL_WIDTH)[:, :TOK_DEV].reshape(TOKENS, MODEL_WIDTH).astype(jnp.bfloat16)
```

```python
import functools

import jax
import jax.numpy as jnp
from jax import lax
from jax.experimental import pallas as pl
from jax.experimental.pallas import tpu as pltpu
from jax.sharding import PartitionSpec as P

ADAPTER_RANK = 16
DOUBLE_RANK = 2 * ADAPTER_RANK
CAP = 28
SLOT = 32
GROUP = 8
BF16 = jnp.bfloat16
F32 = jnp.float32
VMEM_BYTES = 56 * 1024 * 1024
ORDER = (0, 2, 4, 6, 1, 3, 5, 7)


def params(**more):
    return pltpu.CompilerParams(vmem_limit_bytes=VMEM_BYTES, **more)


def full_spec(shape):
    return pl.BlockSpec(shape, lambda *_: (0,) * len(shape))


def slots_kernel(units, scalar_ref, *refs):
    metas, (pick_ref, place_ref, gain_ref) = refs[:-3], refs[-3:]
    metas = [m.at[n] for m in metas for n in range(m.shape[0])]
    rows = max(units, 8)
    topk = metas[0].shape[0]
    tokens = metas[0].shape[1] // 4
    first = scalar_ref[0]
    expert = (lax.broadcasted_iota(jnp.int32, (rows, tokens), 0) + first).astype(F32)
    token = lax.broadcasted_iota(jnp.int32, (rows, tokens), 1)
    slot = lax.broadcasted_iota(jnp.int32, (units, SLOT, tokens), 1).astype(F32)
    before = (
        lax.broadcasted_iota(jnp.int32, (tokens, tokens), 0)
        < lax.broadcasted_iota(jnp.int32, (tokens, tokens), 1)
    ).astype(BF16)
    for r in range(GROUP):
        live = token < scalar_ref[1 + r]
        meta = metas[r][...].astype(F32)
        ids = meta[:, :tokens]
        weights = meta[:, tokens : 2 * tokens] + meta[:, 2 * tokens : 3 * tokens] + meta[:, 3 * tokens :]
        hit = jnp.zeros((rows, tokens), F32)
        gain = jnp.zeros((rows, tokens), F32)
        for k in range(topk):
            same = jnp.broadcast_to(ids[k : k + 1], (rows, tokens)) == expert
            hit = hit + jnp.where(same, 1.0, 0.0)
            gain = gain + jnp.where(same, jnp.broadcast_to(weights[k : k + 1], (rows, tokens)), 0.0)
        hit = jnp.where(live, hit, 0.0)
        position = jnp.dot(hit.astype(BF16), before, preferred_element_type=F32)
        position = jnp.where(hit > 0.5, position, -1.0)[:units]
        pick = jnp.where(jnp.broadcast_to(position[:, None, :], slot.shape) == slot, 1.0, 0.0)
        gains = jnp.sum(pick * gain[:units][:, None, :], axis=2, keepdims=True)
        gain_ref[:, r * SLOT : (r + 1) * SLOT, :] = jnp.broadcast_to(gains, (units, SLOT, 128))
        pick = pick.reshape(units * SLOT, tokens)
        pick_ref[r] = pick.astype(BF16)
        place_ref[r] = pick.T.astype(BF16)


def make_slots(metas, specs, tokens, first_expert, lengths_rel, units):
    scalars = jnp.concatenate([first_expert[None], lengths_rel]).astype(jnp.int32)
    slots = units * SLOT
    return pl.pallas_call(
        functools.partial(slots_kernel, units),
        grid_spec=pltpu.PrefetchScalarGridSpec(
            num_scalar_prefetch=1,
            grid=(1,),
            in_specs=specs,
            out_specs=[
                full_spec((GROUP, slots, tokens)),
                full_spec((GROUP, tokens, slots)),
                full_spec((units, GROUP * SLOT, 128)),
            ],
        ),
        out_shape=[
            jax.ShapeDtypeStruct((GROUP, slots, tokens), BF16),
            jax.ShapeDtypeStruct((GROUP, tokens, slots), BF16),
            jax.ShapeDtypeStruct((units, GROUP * SLOT, 128), F32),
        ],
        compiler_params=params(),
        cost_estimate=pl.CostEstimate(flops=100_000_000, bytes_accessed=4_500_000, transcendentals=0),
    )(scalars, *metas)


def expand_kernel(units, block, quarters, layout, final, scalar_ref, *refs):
    count = len(layout)
    groups, refs = refs[: quarters * count], refs[quarters * count :]
    if final:
        pick_ref, gate_ref, up_ref, start_ref, low_ref, table_ref = refs[:6]
        hidden_ref, gathered, total = refs[6:]
    else:
        pick_ref, gate_ref, up_ref = refs[:3]
        total, gathered = refs[3:]
    q, b = pl.program_id(0), pl.program_id(1)
    tokens, wide = pick_ref.shape[2], gathered.shape[2]
    for turn in range(quarters):

        @pl.when(jnp.logical_and(q == turn, b == 0))
        def _(turn=turn):
            for source, places in zip(groups[turn * count : (turn + 1) * count], layout, strict=True):
                for n, r in enumerate(places):
                    block_rows = source[n] if len(source.shape) == 3 else source[...]
                    rows = jnp.dot(pick_ref[r], block_rows[:tokens], preferred_element_type=F32)
                    gathered[:, r * SLOT : (r + 1) * SLOT, :] = rows.astype(BF16).reshape(units, SLOT, wide)

    if final:

        @pl.when(jnp.logical_and(q == 0, b == 0))
        def _():
            for r in range(GROUP):
                low = lax.dot_general(
                    pick_ref[r], low_ref[r], (((1,), (1,)), ((), ())), preferred_element_type=F32
                ).astype(BF16)
                table = table_ref[scalar_ref[1 + r]]
                added = jnp.dot(low, table, preferred_element_type=F32)
                part = slice(r * SLOT, (r + 1) * SLOT)
                total[:, part, :] = start_ref[:, part, :] + added.reshape(units, SLOT, added.shape[1])

    for e in range(block):
        unit = b * block + e
        both = jnp.concatenate([gate_ref[e], up_ref[e]], axis=1)
        product = jnp.dot(gathered[unit], both, preferred_element_type=F32)
        if not final:

            @pl.when(q == 0)
            def _():
                total[unit] = product

            @pl.when(q > 0)
            def _():
                total[unit] += product

        else:
            value = total[unit] + product

            @pl.when(q < quarters - 1)
            def _():
                total[unit] = value

            @pl.when(q == quarters - 1)
            def _():
                half = value.shape[1] // 2
                gate, up = value[:, :half], value[:, half:]
                hidden_ref[e] = (gate / (1.0 + jnp.exp(-gate)) * up).astype(BF16)


def expand(sources, specs, layout, first, scalars, pick, gate_weight, up_weight, final=None):
    units, width, share = gate_weight.shape
    wide = width // 4
    quarters = len(sources) // len(layout)
    block = min(units, 4)
    rows = GROUP * SLOT
    weight_spec = pl.BlockSpec((block, wide, share), lambda q, b, s: (b, s[0] ^ (q + first), 0))
    in_specs = list(specs) + [full_spec(pick.shape), weight_spec, weight_spec]
    args = list(sources) + [pick, gate_weight, up_weight]
    gathered = pltpu.VMEM((units, rows, wide), BF16)
    total = (units, rows, 2 * share)
    if final is None:
        out_specs = full_spec(total)
        out_shape = jax.ShapeDtypeStruct(total, F32)
        scratch = [gathered]
    else:
        args += list(final)
        in_specs += [full_spec(a.shape) for a in final]
        out_specs = pl.BlockSpec((block, rows, share), lambda q, b, s: (jnp.where(q == quarters - 1, b, 0), 0, 0))
        out_shape = jax.ShapeDtypeStruct((units, rows, share), BF16)
        scratch = [gathered, pltpu.VMEM(total, F32)]
    flops = 2 * quarters * units * rows * wide * (2 * share + 128)
    return pl.pallas_call(
        functools.partial(expand_kernel, units, block, quarters, layout, final is not None),
        grid_spec=pltpu.PrefetchScalarGridSpec(
            num_scalar_prefetch=1,
            grid=(quarters, units // block),
            in_specs=in_specs,
            out_specs=out_specs,
            scratch_shapes=scratch,
        ),
        out_shape=out_shape,
        compiler_params=params(),
        cost_estimate=pl.CostEstimate(
            flops=flops, bytes_accessed=quarters * (units * wide * share * 4 + 2**20) + 2**22, transcendentals=0
        ),
    )(scalars, *args)


def contract_kernel(units, scalar_ref, hidden_ref, down_ref, place_ref, gain_ref, send_ref, keep_ref, table):
    step = pl.program_id(0)
    wide = table.shape[2]
    for e in range(units):
        rows = lax.dot_general(
            hidden_ref[e], down_ref[e], (((1,), (1,)), ((), ())), preferred_element_type=F32
        )
        gain = jnp.concatenate([gain_ref[e]] * (wide // 128), axis=1)
        table[:, e * SLOT : (e + 1) * SLOT, :] = (rows * gain).astype(BF16).reshape(GROUP, SLOT, wide)

    @pl.when(step % 2 == 0)
    def _():
        for r in range(GROUP):
            send_ref[0, r] = jnp.dot(place_ref[r], table[r], preferred_element_type=F32).astype(BF16)

    @pl.when(step % 2 == 1)
    def _():
        for r in range(GROUP):
            keep_ref[0, r] = jnp.dot(place_ref[r], table[r], preferred_element_type=F32)


def contract(hidden, down_weight, place, gain, scalars, part, parts):
    units, width, share = down_weight.shape
    rows = GROUP * SLOT
    tokens = place.shape[1]
    wide = width // 4 // parts
    out = (2, GROUP, tokens, wide)
    out_spec = pl.BlockSpec((1, GROUP, tokens, wide), lambda q, s: (1 - q // 2, 0, 0, 0))
    return pl.pallas_call(
        functools.partial(contract_kernel, units),
        grid_spec=pltpu.PrefetchScalarGridSpec(
            num_scalar_prefetch=1,
            grid=(4,),
            in_specs=[
                full_spec(hidden.shape),
                pl.BlockSpec((units, wide, share), lambda q, s: (0, (s[0] ^ (3 - q)) * parts + part, 0)),
                full_spec(place.shape),
                full_spec(gain.shape),
            ],
            out_specs=[out_spec, out_spec],
            scratch_shapes=[pltpu.VMEM((GROUP, units * SLOT, wide), BF16)],
        ),
        out_shape=[jax.ShapeDtypeStruct(out, BF16), jax.ShapeDtypeStruct(out, F32)],
        compiler_params=params(),
        cost_estimate=pl.CostEstimate(
            flops=8 * units * wide * (rows * share + GROUP * SLOT * tokens),
            bytes_accessed=4 * wide * (units * share * 2 + GROUP * tokens * 3) + 2**21,
            transcendentals=0,
        ),
    )(scalars, hidden, down_weight, place, gain)


def xor_move(value, axis, bits):
    size = lax.axis_size(axis)
    return lax.ppermute(value, axis, [(i, i ^ bits) for i in range(size)])


def every_request(value, axis="dp"):
    blocks, found = value[None], [0]
    for bits in (4, 2, 1):
        blocks = jnp.concatenate([blocks, xor_move(blocks, axis, bits)], axis=0)
        found = found + [f ^ bits for f in found]
    return [blocks[found.index(n)] for n in range(8)]


def select_adapters(request_adapter, rows_local, row_index):
    wanted = request_adapter[:, None] * DOUBLE_RANK + jnp.arange(DOUBLE_RANK)[None, :]
    held = row_index * rows_local + jnp.arange(rows_local)
    return (wanted.reshape(-1)[:, None] == held[None, :]).astype(BF16)


def nt_dot(a, b):
    return lax.dot_general(a, b, (((1,), (1,)), ((), ())), preferred_element_type=F32)


def widen_tables(tables):
    is_gate = (jnp.arange(DOUBLE_RANK) < ADAPTER_RANK)[None, :, None]
    zero = jnp.zeros_like(tables)
    return jnp.concatenate([jnp.where(is_gate, tables, zero), jnp.where(is_gate, zero, tables)], axis=2)


def meta_of(token_experts, router_weight):
    left = router_weight.T
    terms = []
    for _ in range(3):
        term = lax.reduce_precision(left, 8, 7)
        terms.append(term.astype(BF16))
        left = left - term
    return jnp.concatenate([token_experts.T.astype(BF16)] + terms, axis=1)


def near_device(
    tokens,
    lengths,
    request_adapter,
    token_experts,
    router_weight,
    gate_weight,
    up_weight,
    down_weight,
    adapter_input_maps,
    adapter_output_maps,
):
    width = tokens.shape[1]
    units = gate_weight.shape[0]
    dp_count = lax.axis_size("dp")
    tp_count = lax.axis_size("tensor")
    i = lax.axis_index("dp")
    j = lax.axis_index("tensor")
    experts_all = units * dp_count // 2
    quarter = width // tp_count
    rel = i ^ jnp.array(ORDER, jnp.int32)
    tok_rows = tokens.shape[0]
    own = lax.dynamic_slice_in_dim(tokens, j * quarter, quarter, 1)

    block = jnp.concatenate([own, meta_of(token_experts, router_weight)], axis=0)
    ahead = [xor_move(block, "dp", n) for n in (1, 2, 4, 6)]
    behind = xor_move(jnp.stack(ahead[1:]), "dp", 1)
    ahead = jnp.stack(ahead)
    layout = ((0,), (4, 1, 2, 3), (5, 6, 7))

    natural = i ^ jnp.arange(dp_count)
    adapters = jnp.sum(
        jnp.where(natural[:, None] == jnp.arange(dp_count)[None, :], request_adapter[None, :], 0), axis=1
    )
    columns = nt_dot(select_adapters(adapters, adapter_input_maps.shape[1], i), adapter_input_maps)
    columns = columns.astype(BF16)
    for bits in (4, 2, 1):
        mine, theirs = columns[: bits * DOUBLE_RANK], columns[bits * DOUBLE_RANK :]
        columns = mine + xor_move(theirs, "dp", bits)
    low = nt_dot(columns, own)
    low = low + xor_move(low, "tensor", 1)
    low = low + xor_move(low, "tensor", 2)
    low = every_request(low.astype(BF16))
    low = jnp.stack([low[n] for n in ORDER])

    halves = adapter_output_maps.reshape(adapter_output_maps.shape[0], -1)
    tables = jnp.dot(
        select_adapters(request_adapter, halves.shape[0], i), halves, preferred_element_type=F32
    ).astype(BF16)
    share = halves.shape[1] // 2
    upper = i >= dp_count // 2
    low_half, high_half = tables[:, :share], tables[:, share:]
    tables = jnp.where(upper, high_half, low_half) + xor_move(
        jnp.where(upper, low_half, high_half), "dp", 4
    )
    for bits in (2, 1):
        tables = tables + xor_move(tables, "dp", bits)
    tables = widen_tables(tables.reshape(dp_count, DOUBLE_RANK, share))

    core_ahead, core_behind = xor_move(ahead, "tensor", 1), xor_move(behind, "tensor", 1)
    side_ahead, side_behind = xor_move(ahead, "tensor", 2), xor_move(behind, "tensor", 2)
    both_ahead, both_behind = xor_move(side_ahead, "tensor", 1), xor_move(side_behind, "tensor", 1)

    is_rel = rel[:, None] == jnp.arange(dp_count)[None, :]
    lengths_rel = jnp.sum(jnp.where(is_rel, lengths[None, :], 0), axis=1)
    first_expert = (i * units) % experts_all
    routes = block.shape[0] - tok_rows
    meta_specs = [
        pl.BlockSpec((n, routes, quarter), lambda *_: (0, tok_rows // routes, 0)) for n in (1, 3, 1, 3)
    ]
    meta_specs[2] = pl.BlockSpec((1, routes, quarter), lambda *_: (0, tok_rows // routes, 0))
    meta_specs[1] = pl.BlockSpec((3, routes, quarter), lambda *_: (0, tok_rows // routes, 0))
    pick, place, gain = make_slots(
        [block[None], ahead[1:], ahead[:1], behind], meta_specs, tok_rows, first_expert, lengths_rel, units
    )

    scalars = jnp.concatenate([j[None], rel]).astype(jnp.int32)

    def own_spec(q0):
        return pl.BlockSpec((tok_rows, quarter), lambda *a: (0, a[-1][0] ^ q0))

    def sources(*pairs):
        return [x for pair in pairs for x in (tokens,) + pair]

    def specs(first, *pairs):
        return [
            s
            for n, pair in enumerate(pairs)
            for s in [own_spec(first + n)] + [full_spec(x.shape) for x in pair]
        ]

    pairs = [(ahead, behind), (core_ahead, core_behind), (side_ahead, side_behind), (both_ahead, both_behind)]
    start = expand(
        sources(*pairs[:2]), specs(0, *pairs[:2]), layout, 0, scalars, pick, gate_weight, up_weight
    )
    hidden = expand(
        sources(*pairs[2:]),
        specs(2, *pairs[2:]),
        layout,
        2,
        scalars,
        pick,
        gate_weight,
        up_weight,
        (start, low, tables),
    )

    results = []
    parts = 2
    for part in range(parts):
        send, keep = contract(hidden, down_weight, place, gain, scalars, part, parts)
        sums = keep + xor_move(send, "tensor", 1).astype(F32)
        if part % 2 == 0:
            here = sums[0] + xor_move(sums[1].astype(BF16), "tensor", 2).astype(F32)
            here = here[:4] + xor_move(here[4:].astype(BF16), "dp", 1).astype(F32)
        else:
            sums = sums[:, :4] + xor_move(sums[:, 4:].astype(BF16), "dp", 1).astype(F32)
            here = sums[0] + xor_move(sums[1].astype(BF16), "tensor", 2).astype(F32)
        last = here[0]
        for k in (1, 2, 3):
            last = last + xor_move(here[k].astype(BF16), "dp", 2 * k).astype(F32)
        results.append(last.astype(BF16))
    return jnp.concatenate(results, axis=1)


def any_device(
    tokens,
    lengths,
    request_adapter,
    token_experts,
    router_weight,
    gate_weight,
    up_weight,
    down_weight,
    adapter_input_maps,
    adapter_output_maps,
):
    tok_rows, width = tokens.shape
    units = gate_weight.shape[0]
    dp_count = lax.axis_size("dp")
    tp_count = lax.axis_size("tensor")
    i = lax.axis_index("dp")
    j = lax.axis_index("tensor")
    experts_all = units * dp_count // 2
    quarter = width // tp_count
    meta = lax.all_gather(meta_of(token_experts, router_weight), "dp", axis=0)
    rows = lax.all_gather(tokens, "dp", axis=0)
    maps = lax.all_gather(adapter_input_maps, "dp", axis=1, tiled=True)
    adapter = jnp.sum(jnp.where(jnp.arange(dp_count) == i, request_adapter, 0))
    columns = nt_dot(select_adapters(adapter[None], maps.shape[1], 0), maps).astype(BF16)
    x_part = lax.dynamic_slice_in_dim(tokens, j * quarter, quarter, 1)
    low = lax.psum(nt_dot(columns, x_part), "tensor").astype(BF16)
    low = lax.all_gather(low, "dp", axis=0)
    every = lax.all_gather(adapter_output_maps, "dp", axis=0, tiled=True)
    half = jnp.where(i * units >= experts_all, every[:, 1], every[:, 0])
    tables = jnp.dot(
        select_adapters(request_adapter, half.shape[0], 0), half, preferred_element_type=F32
    ).astype(BF16)
    tables = widen_tables(tables.reshape(dp_count, DOUBLE_RANK, half.shape[1]))
    first_expert = (i * units) % experts_all
    natural = jnp.concatenate([j[None], jnp.arange(GROUP)]).astype(jnp.int32)

    def one_group(group):
        meta_g, rows_g, low_g, tables_g, lengths_g = group
        pick, place, gain = make_slots(
            [meta_g], [full_spec(meta_g.shape)], tok_rows, first_expert, lengths_g, units
        )
        layout = (tuple(range(GROUP)),)

        def spec(q0):
            return pl.BlockSpec((GROUP, tok_rows, quarter), lambda *a: (0, 0, a[-1][0] ^ q0))

        start = expand(
            [rows_g] * 2, [spec(0), spec(1)], layout, 0, natural, pick, gate_weight, up_weight
        )
        hidden = expand(
            [rows_g] * 2,
            [spec(2), spec(3)],
            layout,
            2,
            natural,
            pick,
            gate_weight,
            up_weight,
            (start, low_g, tables_g),
        )
        send, keep = contract(hidden, down_weight, place, gain, natural, 0, 1)
        return keep.astype(BF16), send

    groups = dp_count // GROUP
    grouped = [
        a.reshape((groups, GROUP) + a.shape[1:]) for a in (meta, rows, low, tables, lengths)
    ]
    keep, send = lax.map(one_group, tuple(grouped))
    sums = [keep[:, 0], send[:, 0], keep[:, 1], send[:, 1]]
    sums = [a.reshape(dp_count * tok_rows, quarter) for a in sums]
    here = sums[0].astype(F32)
    for q in range(1, 4):
        here = here + xor_move(sums[q], "tensor", q).astype(F32)
    return lax.psum_scatter(here, "dp", scatter_dimension=0, tiled=True).astype(BF16)


def solution(mesh):
    near = mesh.shape["dp"] == 8 and mesh.shape["tensor"] == 4
    in_specs = (
        P("dp", None),
        P(),
        P(),
        P("dp", None),
        P("dp", None),
        P("dp", None, "tensor"),
        P("dp", None, "tensor"),
        P("dp", None, "tensor"),
        P("tensor", "dp"),
        P("dp", None, "tensor"),
    )
    return jax.shard_map(
        near_device if near else any_device,
        mesh=mesh,
        in_specs=in_specs,
        out_specs=P("dp", "tensor"),
        check_vma=False,
    )
```

```python
import functools

import jax
import jax.numpy as jnp
from jax import lax
from jax.experimental import pallas as pl
from jax.experimental.pallas import tpu as pltpu
from jax.sharding import PartitionSpec as P

ADAPTER_RANK = 16
DOUBLE_RANK = 2 * ADAPTER_RANK
CAP = 28
SLOT = 32
GROUP = 8
BF16 = jnp.bfloat16
F32 = jnp.float32
VMEM_BYTES = 12 * 1024 * 1024
EXPAND_BYTES = 46 * 1024 * 1024
UNROLL = 16
COST = pl.CostEstimate(flops=1_000_000, bytes_accessed=1_000, transcendentals=0)
ORDER = (0, 2, 4, 6, 1, 3, 5, 7)
HALVING = (0, 4, 2, 6, 1, 5, 3, 7)


def params(size=VMEM_BYTES):
    return pltpu.CompilerParams(vmem_limit_bytes=size)


def full_spec(shape):
    return pl.BlockSpec(shape, lambda *_: (0,) * len(shape))


def nt_dot(a, b):
    return lax.dot_general(a, b, (((1,), (1,)), ((), ())), preferred_element_type=F32)


def slots_kernel(units, scalar_ref, *refs):
    metas, (pick_ref, place_ref, gain_ref) = refs[:-3], refs[-3:]
    metas = [m.at[n] for m in metas for n in range(m.shape[0])]
    rows = max(units, 8)
    topk = metas[0].shape[0]
    tokens = metas[0].shape[1] // 4
    first = scalar_ref[0]
    expert = (lax.broadcasted_iota(jnp.int32, (rows, tokens), 0) + first).astype(F32)
    token = lax.broadcasted_iota(jnp.int32, (rows, tokens), 1)
    slot = lax.broadcasted_iota(jnp.int32, (units, SLOT, tokens), 1).astype(F32)
    before = (
        lax.broadcasted_iota(jnp.int32, (tokens, tokens), 0)
        < lax.broadcasted_iota(jnp.int32, (tokens, tokens), 1)
    ).astype(BF16)
    for r in range(GROUP):
        live = token < scalar_ref[1 + r]
        meta = metas[r][...].astype(F32)
        ids = meta[:, :tokens]
        weights = meta[:, tokens : 2 * tokens] + meta[:, 2 * tokens : 3 * tokens] + meta[:, 3 * tokens :]
        hit = jnp.zeros((rows, tokens), F32)
        gain = jnp.zeros((rows, tokens), F32)
        for k in range(topk):
            same = jnp.broadcast_to(ids[k : k + 1], (rows, tokens)) == expert
            hit = hit + jnp.where(same, 1.0, 0.0)
            gain = gain + jnp.where(same, jnp.broadcast_to(weights[k : k + 1], (rows, tokens)), 0.0)
        hit = jnp.where(live, hit, 0.0)
        position = jnp.dot(hit.astype(BF16), before, preferred_element_type=F32)
        position = jnp.where(hit > 0.5, position, -1.0)[:units]
        pick = jnp.where(jnp.broadcast_to(position[:, None, :], slot.shape) == slot, 1.0, 0.0)
        gains = jnp.sum(pick * gain[:units][:, None, :], axis=2, keepdims=True)
        gain_ref[:, r * SLOT : (r + 1) * SLOT, :] = jnp.broadcast_to(gains, (units, SLOT, 128))
        pick = pick.reshape(units * SLOT, tokens)
        pick_ref[r] = pick.astype(BF16)
        place_ref[r] = pick.T.astype(BF16)


def make_slots(metas, specs, tokens, scalars, units):
    slots = units * SLOT
    return pl.pallas_call(
        functools.partial(slots_kernel, units),
        grid_spec=pltpu.PrefetchScalarGridSpec(
            num_scalar_prefetch=1,
            grid=(1,),
            in_specs=specs,
            out_specs=[
                full_spec((GROUP, slots, tokens)),
                full_spec((GROUP, tokens, slots)),
                full_spec((units, GROUP * SLOT, 128)),
            ],
        ),
        out_shape=[
            jax.ShapeDtypeStruct((GROUP, slots, tokens), BF16),
            jax.ShapeDtypeStruct((GROUP, tokens, slots), BF16),
            jax.ShapeDtypeStruct((units, GROUP * SLOT, 128), F32),
        ],
        compiler_params=params(),
        cost_estimate=COST,
    )(scalars, *metas)


def expand_kernel(units, quarters, first, layout, final, scalar_ref, *refs):
    count = len(layout)
    groups, refs = refs[: quarters * count], refs[quarters * count :]
    if final:
        pick_ref, gate_hbm, up_hbm, start_ref, low_ref, table_ref = refs[:6]
        out_ref, gathered, both_ref, done, low_rows, tables = refs[6:]
    else:
        pick_ref, gate_hbm, up_hbm, out_ref, gathered, both_ref, done = refs
    tokens, wide = pick_ref.shape[2], gathered.shape[3]
    places = [slice(r * SLOT, (r + 1) * SLOT) for r in range(GROUP)]
    at = [
        pl.ds(pl.multiple_of((scalar_ref[0] ^ (first + turn)) * wide, wide), wide)
        for turn in range(quarters)
    ]

    block = min(units, 4)
    copies = []
    for g in range(units // block):
        part = pl.ds(g * block, block)
        for turn in range(quarters):
            for n, weight in enumerate((gate_hbm, up_hbm)):
                copy = pltpu.make_async_copy(
                    weight.at[part, at[turn], :], both_ref.at[turn, n, part], done.at[g, turn, n]
                )
                copy.start()
                copies.append(copy)

    def scatter(target, r, rows):
        target[:, places[r], :] = rows.astype(BF16).reshape(units, SLOT, rows.shape[1])

    for turn in range(quarters):
        for source, spots in zip(groups[turn * count : (turn + 1) * count], layout, strict=True):
            for n, r in enumerate(spots):
                if len(source.shape) == 2:
                    block_rows = source[:, at[turn]]
                elif source.shape[2] == wide:
                    block_rows = source[n, :tokens, :]
                else:
                    block_rows = source[n, :, at[turn]]
                scatter(gathered.at[turn], r, jnp.dot(pick_ref[r], block_rows, preferred_element_type=F32))
    if final:
        zero = jnp.zeros((SLOT, tokens), BF16)
        for r in range(GROUP):
            spread = jnp.concatenate([zero] * r + [low_ref[r]] + [zero] * (GROUP - 1 - r), axis=0)
            scatter(low_rows, r, nt_dot(pick_ref[r], spread))
            tables[places[r], :] = table_ref[scalar_ref[1 + r]]

    def one(unit, carry):
        value = None
        for turn in range(quarters):
            both = jnp.concatenate([both_ref[turn, 0, unit], both_ref[turn, 1, unit]], axis=1)
            product = jnp.dot(gathered[turn, unit], both, preferred_element_type=F32)
            value = product if value is None else value + product
        if final:
            value = value + jnp.dot(low_rows[unit], tables[...], preferred_element_type=F32)
            value = value + start_ref[unit]
            half = value.shape[1] // 2
            gate, up = value[:, :half], value[:, half:]
            out_ref[unit] = (gate / (1.0 + jnp.exp(-gate)) * up).astype(BF16)
        else:
            out_ref[unit] = value
        return carry

    for g in range(units // block):
        for copy in copies[g * 2 * quarters : (g + 1) * 2 * quarters]:
            copy.wait()
        lax.fori_loop(g * block, (g + 1) * block, one, 0, unroll=block)


def expand(sources, layout, first, scalars, pick, gate_weight, up_weight, final=None):
    units, width, share = gate_weight.shape
    wide = width // 4
    quarters = len(sources) // len(layout)
    rows = GROUP * SLOT
    args = list(sources) + [pick, gate_weight, up_weight]
    scratch = [
        pltpu.VMEM((quarters, units, rows, wide), BF16),
        pltpu.VMEM((quarters, 2, units, wide, share), BF16),
        pltpu.SemaphoreType.DMA((units, quarters, 2)),
    ]
    if final is None:
        out_shape = jax.ShapeDtypeStruct((units, rows, 2 * share), F32)
    else:
        args += list(final)
        out_shape = jax.ShapeDtypeStruct((units, rows, share), BF16)
        scratch += [pltpu.VMEM((units, rows, rows), BF16), pltpu.VMEM((rows, 2 * share), BF16)]
    count = len(sources) + 1
    vmem = pl.BlockSpec(memory_space=pltpu.VMEM)
    hbm = pl.BlockSpec(memory_space=pl.ANY)
    return pl.pallas_call(
        functools.partial(expand_kernel, units, quarters, first, layout, final is not None),
        in_specs=[pl.BlockSpec(memory_space=pltpu.SMEM)] + [vmem] * count + [hbm, hbm] + [vmem] * (len(args) - count - 2),
        out_specs=vmem,
        scratch_shapes=scratch,
        out_shape=out_shape,
        compiler_params=params(EXPAND_BYTES),
        cost_estimate=COST,
    )(scalars, *args)


def contract_kernel(units, jobs, parts, scalar_ref, down_hbm, hidden_ref, place_ref, gain_ref, *refs):
    outs, (table, down_ref, done) = refs[:-3], refs[-3:]
    wide = table.shape[2]
    copies = []
    for n, (part, q) in enumerate(jobs):
        at = pl.ds(pl.multiple_of(((scalar_ref[0] ^ q) * parts + part) * wide, wide), wide)
        copies.append(pltpu.make_async_copy(down_hbm.at[:, at, :], down_ref.at[n], done.at[n]))
        copies[n].start()
    for n in range(len(jobs)):
        copies[n].wait()

        def one(unit, carry, n=n):
            rows = nt_dot(hidden_ref[unit], down_ref[n, unit])
            gain = jnp.concatenate([gain_ref[unit]] * (wide // 128), axis=1)
            spot = pl.ds(pl.multiple_of(unit * SLOT, SLOT), SLOT)
            table[:, spot, :] = (rows * gain).astype(BF16).reshape(GROUP, SLOT, wide)
            return carry

        lax.fori_loop(0, units, one, 0, unroll=min(units, UNROLL))
        for r in range(GROUP):
            sums = jnp.dot(place_ref[r], table[r], preferred_element_type=F32)
            outs[n][r] = sums.astype(outs[n].dtype)


def contract(hidden, down_weight, place, gain, scalars, jobs, parts):
    units, width, share = down_weight.shape
    tokens = place.shape[1]
    wide = width // 4 // parts
    vmem = pl.BlockSpec(memory_space=pltpu.VMEM)
    return pl.pallas_call(
        functools.partial(contract_kernel, units, jobs, parts),
        in_specs=[pl.BlockSpec(memory_space=pltpu.SMEM), pl.BlockSpec(memory_space=pl.ANY)] + [vmem] * 3,
        out_specs=[vmem] * len(jobs),
        scratch_shapes=[
            pltpu.VMEM((GROUP, units * SLOT, wide), BF16),
            pltpu.VMEM((len(jobs), units, wide, share), BF16),
            pltpu.SemaphoreType.DMA((len(jobs),)),
        ],
        out_shape=[jax.ShapeDtypeStruct((GROUP, tokens, wide), BF16 if q % 2 else F32) for _, q in jobs],
        compiler_params=params(EXPAND_BYTES),
        cost_estimate=COST,
    )(scalars, down_weight, hidden, place, gain)


def xor_move(value, axis, bits):
    size = lax.axis_size(axis)
    return lax.ppermute(value, axis, [(i, i ^ bits) for i in range(size)])


def every_request(value, axis="dp"):
    blocks, found = value[None], [0]
    for bits in (4, 2, 1):
        blocks = jnp.concatenate([blocks, xor_move(blocks, axis, bits)], axis=0)
        found = found + [f ^ bits for f in found]
    return [blocks[found.index(n)] for n in range(8)]


def select_adapters(request_adapter, rows_local, row_index):
    wanted = request_adapter[:, None] * DOUBLE_RANK + jnp.arange(DOUBLE_RANK)[None, :]
    held = row_index * rows_local + jnp.arange(rows_local)
    return (wanted.reshape(-1)[:, None] == held[None, :]).astype(BF16)


def widen_tables(tables):
    is_gate = (jnp.arange(DOUBLE_RANK) < ADAPTER_RANK)[None, :, None]
    zero = jnp.zeros_like(tables)
    return jnp.concatenate([jnp.where(is_gate, tables, zero), jnp.where(is_gate, zero, tables)], axis=2)


def meta_of(token_experts, router_weight):
    left = router_weight.T
    terms = []
    for _ in range(3):
        term = lax.reduce_precision(left, 8, 7)
        terms.append(term.astype(BF16))
        left = left - term
    return jnp.concatenate([token_experts.T.astype(BF16)] + terms, axis=1)


def end_along_z(here):
    last = here[0]
    for k in (1, 2, 3):
        last = last + xor_move(here[k].astype(BF16), "dp", 2 * k).astype(F32)
    return last.astype(BF16)


def near_device(
    tokens,
    lengths,
    request_adapter,
    token_experts,
    router_weight,
    gate_weight,
    up_weight,
    down_weight,
    adapter_input_maps,
    adapter_output_maps,
):
    width = tokens.shape[1]
    units = gate_weight.shape[0]
    dp_count = lax.axis_size("dp")
    tp_count = lax.axis_size("tensor")
    i = lax.axis_index("dp")
    j = lax.axis_index("tensor")
    experts_all = units * dp_count // 2
    quarter = width // tp_count
    rel = i ^ jnp.array(ORDER, jnp.int32)
    tok_rows = tokens.shape[0]
    own = lax.dynamic_slice_in_dim(tokens, j * quarter, quarter, 1)

    block = jnp.concatenate([own, meta_of(token_experts, router_weight)], axis=0)
    ahead = [xor_move(block, "dp", n) for n in (1, 2, 4, 6)]
    layout = ((0,), (4, 1, 2, 3), (5, 6, 7))

    natural = i ^ jnp.array(HALVING, jnp.int32)
    adapters = jnp.sum(
        jnp.where(natural[:, None] == jnp.arange(dp_count)[None, :], request_adapter[None, :], 0), axis=1
    )
    columns = nt_dot(select_adapters(adapters, adapter_input_maps.shape[1], i), adapter_input_maps)
    columns = columns.astype(BF16)

    halves = adapter_output_maps.reshape(adapter_output_maps.shape[0], -1)
    tables = jnp.dot(
        select_adapters(request_adapter, halves.shape[0], i), halves, preferred_element_type=F32
    ).astype(BF16)
    share = halves.shape[1] // 2
    upper = i >= dp_count // 2
    first_expert = (i * units) % experts_all
    is_rel = rel[:, None] == jnp.arange(dp_count)[None, :]
    lengths_rel = jnp.sum(jnp.where(is_rel, lengths[None, :], 0), axis=1)
    slot_scalars = jnp.concatenate([first_expert[None], lengths_rel]).astype(jnp.int32)
    scalars = jnp.concatenate([j[None], rel]).astype(jnp.int32)
    strips = quarter // share

    def strip(rows):
        return [rows[:, n * share : (n + 1) * share] for n in range(rows.shape[1] // share)]

    def halve(columns, given, bits):
        kept = columns.shape[0] // 2
        got = xor_move(jnp.concatenate(strip(columns[kept:]) + given, axis=0), "dp", bits)
        more = jnp.concatenate([got[n * kept : (n + 1) * kept] for n in range(strips)], axis=1)
        got = got[strips * kept :]
        size = given[0].shape[0]
        return columns[:kept] + more, [got[n * size : (n + 1) * size] for n in range(len(given))]

    tables = strip(tables)
    for bits in (1, 2):
        columns, came = halve(columns, tables, bits)
        tables = [t + c for t, c in zip(tables, came, strict=True)]
    mine, other = jnp.where(upper, tables[1], tables[0]), jnp.where(upper, tables[0], tables[1])

    ahead, columns, mine, other = lax.optimization_barrier((ahead, columns, mine, other))
    behind = xor_move(jnp.stack(ahead[1:]), "dp", 1)
    ahead = jnp.stack(ahead)
    side_ahead = xor_move(ahead, "tensor", 2)
    core_ahead = xor_move(ahead, "tensor", 1)
    columns, came = halve(columns, [other], 4)
    tables = mine + came[0]
    low = nt_dot(columns, own)
    low = low + xor_move(low, "tensor", 1)

    behind, low, tables, side_ahead = lax.optimization_barrier((behind, low, tables, side_ahead))
    low = low + xor_move(low, "tensor", 2)
    side_behind = xor_move(behind, "tensor", 2)
    core_behind = xor_move(behind, "tensor", 1)
    low = every_request(low.astype(BF16))
    low = jnp.stack([low[n] for n in ORDER])
    both_ahead = xor_move(side_ahead, "tensor", 1)
    tables = widen_tables(tables.reshape(dp_count, DOUBLE_RANK, share))

    routes = block.shape[0] - tok_rows
    meta_specs = [
        pl.BlockSpec((n, routes, quarter), lambda *_: (0, tok_rows // routes, 0)) for n in (1, 3, 1, 3)
    ]
    meta_specs[2] = pl.BlockSpec((1, routes, quarter), lambda *_: (0, tok_rows // routes, 0))
    meta_specs[1] = pl.BlockSpec((3, routes, quarter), lambda *_: (0, tok_rows // routes, 0))
    pick, place, gain = make_slots(
        [block[None], ahead[1:], ahead[:1], behind], meta_specs, tok_rows, slot_scalars, units
    )

    def sources(*pairs):
        return [x for pair in pairs for x in (tokens,) + pair]

    start = expand(
        sources((ahead, behind), (core_ahead, core_behind)), layout, 0, scalars, pick, gate_weight, up_weight
    )
    start, side_behind = lax.optimization_barrier((start, side_behind))
    both_behind = xor_move(side_behind, "tensor", 1)
    hidden = expand(
        sources((side_ahead, side_behind), (both_ahead, both_behind)),
        layout,
        2,
        scalars,
        pick,
        gate_weight,
        up_weight,
        (start, low, tables),
    )

    def core_sum(send, keep):
        return keep + xor_move(send, "tensor", 1).astype(F32)

    early = contract(hidden, down_weight, place, gain, scalars, ((0, 3), (0, 2)), 2)
    there = core_sum(*early).astype(BF16)
    there, hidden = lax.optimization_barrier((there, hidden))
    late = ((1, 3), (1, 2), (1, 1), (1, 0), (0, 1), (0, 0))
    late = contract(hidden, down_weight, place, gain, scalars, late, 2)

    here = core_sum(*late[4:]) + xor_move(there, "tensor", 2).astype(F32)
    here = here[:4] + xor_move(here[4:].astype(BF16), "dp", 1).astype(F32)
    first = end_along_z(here)

    here, there = core_sum(*late[2:4]), core_sum(*late[:2])
    sums = xor_move(jnp.stack([here[4:].astype(BF16), there[4:].astype(BF16)]), "dp", 1).astype(F32)
    here, there = here[:4] + sums[0], there[:4] + sums[1]
    here = here + xor_move(there.astype(BF16), "tensor", 2).astype(F32)
    second = end_along_z(here)
    return jnp.concatenate([first, second], axis=1)


def any_device(
    tokens,
    lengths,
    request_adapter,
    token_experts,
    router_weight,
    gate_weight,
    up_weight,
    down_weight,
    adapter_input_maps,
    adapter_output_maps,
):
    tok_rows, width = tokens.shape
    units = gate_weight.shape[0]
    dp_count = lax.axis_size("dp")
    tp_count = lax.axis_size("tensor")
    i = lax.axis_index("dp")
    j = lax.axis_index("tensor")
    experts_all = units * dp_count // 2
    quarter = width // tp_count
    meta = lax.all_gather(meta_of(token_experts, router_weight), "dp", axis=0)
    rows = lax.all_gather(tokens, "dp", axis=0)
    maps = lax.all_gather(adapter_input_maps, "dp", axis=1, tiled=True)
    adapter = jnp.sum(jnp.where(jnp.arange(dp_count) == i, request_adapter, 0))
    columns = nt_dot(select_adapters(adapter[None], maps.shape[1], 0), maps).astype(BF16)
    x_part = lax.dynamic_slice_in_dim(tokens, j * quarter, quarter, 1)
    low = lax.psum(nt_dot(columns, x_part), "tensor").astype(BF16)
    low = lax.all_gather(low, "dp", axis=0)
    every = lax.all_gather(adapter_output_maps, "dp", axis=0, tiled=True)
    half = jnp.where(i * units >= experts_all, every[:, 1], every[:, 0])
    tables = jnp.dot(
        select_adapters(request_adapter, half.shape[0], 0), half, preferred_element_type=F32
    ).astype(BF16)
    tables = widen_tables(tables.reshape(dp_count, DOUBLE_RANK, half.shape[1]))
    first_expert = (i * units) % experts_all
    natural = jnp.concatenate([j[None], jnp.arange(GROUP)]).astype(jnp.int32)

    def one_group(group):
        meta_g, rows_g, low_g, tables_g, lengths_g = group
        pick, place, gain = make_slots(
            [meta_g],
            [full_spec(meta_g.shape)],
            tok_rows,
            jnp.concatenate([first_expert[None], lengths_g]).astype(jnp.int32),
            units,
        )
        layout = (tuple(range(GROUP)),)

        start = expand([rows_g] * 2, layout, 0, natural, pick, gate_weight, up_weight)
        hidden = expand(
            [rows_g] * 2, layout, 2, natural, pick, gate_weight, up_weight, (start, low_g, tables_g)
        )
        jobs = tuple((0, q) for q in range(4))
        sums = contract(hidden, down_weight, place, gain, natural, jobs, 1)
        return tuple(a.astype(BF16) for a in sums)

    groups = dp_count // GROUP
    grouped = [
        a.reshape((groups, GROUP) + a.shape[1:]) for a in (meta, rows, low, tables, lengths)
    ]
    sums = lax.map(one_group, tuple(grouped))
    sums = [a.reshape(dp_count * tok_rows, quarter) for a in sums]
    here = sums[0].astype(F32)
    for q in range(1, 4):
        here = here + xor_move(sums[q], "tensor", q).astype(F32)
    return lax.psum_scatter(here, "dp", scatter_dimension=0, tiled=True).astype(BF16)


def solution(mesh):
    near = mesh.shape["dp"] == 8 and mesh.shape["tensor"] == 4
    in_specs = (
        P("dp", None),
        P(),
        P(),
        P("dp", None),
        P("dp", None),
        P("dp", None, "tensor"),
        P("dp", None, "tensor"),
        P("dp", None, "tensor"),
        P("tensor", "dp"),
        P("dp", None, "tensor"),
    )
    return jax.shard_map(
        near_device if near else any_device,
        mesh=mesh,
        in_specs=in_specs,
        out_specs=P("dp", "tensor"),
        check_vma=False,
    )
```

```python
import functools

import jax
import jax.numpy as jnp
from jax import lax
from jax.experimental import pallas as pl
from jax.experimental.pallas import tpu as pltpu
from jax.sharding import PartitionSpec as P

ADAPTER_RANK = 16
DOUBLE_RANK = 2 * ADAPTER_RANK
CAP = 28
SLOT = 32
GROUP = 8
BF16 = jnp.bfloat16
F32 = jnp.float32
VMEM_BYTES = 12 * 1024 * 1024
EXPAND_BYTES = 46 * 1024 * 1024
UNROLL = 16
COST = pl.CostEstimate(flops=1_000_000, bytes_accessed=1_000, transcendentals=0)
ORDER = (0, 2, 4, 6, 1, 3, 5, 7)
HALVING = (0, 4, 2, 6, 1, 5, 3, 7)
GATHERED = (0, 4, 2, 6, 1, 5, 3, 7)


def params(size=VMEM_BYTES):
    return pltpu.CompilerParams(vmem_limit_bytes=size)


def full_spec(shape):
    return pl.BlockSpec(shape, lambda *_: (0,) * len(shape))


def nt_dot(a, b):
    return lax.dot_general(a, b, (((1,), (1,)), ((), ())), preferred_element_type=F32)


def slots_kernel(units, scalar_ref, *refs):
    metas, (pick_ref, place_ref, gain_ref) = refs[:-3], refs[-3:]
    metas = [m.at[n] for m in metas for n in range(m.shape[0])]
    rows = max(units, 8)
    topk = metas[0].shape[0]
    tokens = metas[0].shape[1] // 4
    first = scalar_ref[0]
    expert = (lax.broadcasted_iota(jnp.int32, (rows, tokens), 0) + first).astype(F32)
    token = lax.broadcasted_iota(jnp.int32, (rows, tokens), 1)
    slot = lax.broadcasted_iota(jnp.int32, (units, SLOT, tokens), 1).astype(F32)
    before = (
        lax.broadcasted_iota(jnp.int32, (tokens, tokens), 0)
        < lax.broadcasted_iota(jnp.int32, (tokens, tokens), 1)
    ).astype(BF16)
    for r in range(GROUP):
        live = token < scalar_ref[1 + r]
        meta = metas[r][...].astype(F32)
        ids = meta[:, :tokens]
        weights = meta[:, tokens : 2 * tokens] + meta[:, 2 * tokens : 3 * tokens] + meta[:, 3 * tokens :]
        hit = jnp.zeros((rows, tokens), F32)
        gain = jnp.zeros((rows, tokens), F32)
        for k in range(topk):
            same = jnp.broadcast_to(ids[k : k + 1], (rows, tokens)) == expert
            hit = hit + jnp.where(same, 1.0, 0.0)
            gain = gain + jnp.where(same, jnp.broadcast_to(weights[k : k + 1], (rows, tokens)), 0.0)
        hit = jnp.where(live, hit, 0.0)
        position = jnp.dot(hit.astype(BF16), before, preferred_element_type=F32)
        position = jnp.where(hit > 0.5, position, -1.0)[:units]
        pick = jnp.where(jnp.broadcast_to(position[:, None, :], slot.shape) == slot, 1.0, 0.0)
        gains = jnp.sum(pick * gain[:units][:, None, :], axis=2, keepdims=True)
        gain_ref[:, r * SLOT : (r + 1) * SLOT, :] = jnp.broadcast_to(gains, (units, SLOT, 128))
        pick = pick.reshape(units * SLOT, tokens)
        pick_ref[r] = pick.astype(BF16)
        place_ref[r] = pick.T.astype(BF16)


def make_slots(metas, specs, tokens, scalars, units):
    slots = units * SLOT
    return pl.pallas_call(
        functools.partial(slots_kernel, units),
        grid_spec=pltpu.PrefetchScalarGridSpec(
            num_scalar_prefetch=1,
            grid=(1,),
            in_specs=specs,
            out_specs=[
                full_spec((GROUP, slots, tokens)),
                full_spec((GROUP, tokens, slots)),
                full_spec((units, GROUP * SLOT, 128)),
            ],
        ),
        out_shape=[
            jax.ShapeDtypeStruct((GROUP, slots, tokens), BF16),
            jax.ShapeDtypeStruct((GROUP, tokens, slots), BF16),
            jax.ShapeDtypeStruct((units, GROUP * SLOT, 128), F32),
        ],
        compiler_params=params(),
        cost_estimate=COST,
    )(scalars, *metas)


def expand_kernel(units, quarters, first, layout, final, scalar_ref, *refs):
    count = len(layout)
    groups, refs = refs[: quarters * count], refs[quarters * count :]
    if final:
        pick_ref, gate_hbm, up_hbm, start_ref, low_ref, table_ref = refs[:6]
        out_ref, gathered, both_ref, done, low_rows, tables = refs[6:]
    else:
        pick_ref, gate_hbm, up_hbm, out_ref, gathered, both_ref, done = refs
    tokens, wide = pick_ref.shape[2], gathered.shape[3]
    places = [slice(r * SLOT, (r + 1) * SLOT) for r in range(GROUP)]
    at = [
        pl.ds(pl.multiple_of((scalar_ref[0] ^ (first + turn)) * wide, wide), wide)
        for turn in range(quarters)
    ]

    block = min(units, 4)
    copies = []
    for g in range(units // block):
        part = pl.ds(g * block, block)
        for turn in range(quarters):
            for n, weight in enumerate((gate_hbm, up_hbm)):
                copy = pltpu.make_async_copy(
                    weight.at[part, at[turn], :], both_ref.at[turn, n, part], done.at[g, turn, n]
                )
                copy.start()
                copies.append(copy)

    def scatter(target, r, rows):
        target[:, places[r], :] = rows.astype(BF16).reshape(units, SLOT, rows.shape[1])

    for turn in range(quarters):
        for source, spots in zip(groups[turn * count : (turn + 1) * count], layout, strict=True):
            for n, r in enumerate(spots):
                if len(source.shape) == 2:
                    block_rows = source[:, at[turn]]
                elif source.shape[2] == wide:
                    block_rows = source[n, :tokens, :]
                else:
                    block_rows = source[n, :, at[turn]]
                scatter(gathered.at[turn], r, jnp.dot(pick_ref[r], block_rows, preferred_element_type=F32))
    if final:
        zero = jnp.zeros((SLOT, tokens), BF16)
        for r in range(GROUP):
            spread = jnp.concatenate([zero] * r + [low_ref[r]] + [zero] * (GROUP - 1 - r), axis=0)
            scatter(low_rows, r, nt_dot(pick_ref[r], spread))
            tables[places[r], :] = table_ref[scalar_ref[1 + r]]

    def one(unit, carry):
        value = None
        for turn in range(quarters):
            both = jnp.concatenate([both_ref[turn, 0, unit], both_ref[turn, 1, unit]], axis=1)
            product = jnp.dot(gathered[turn, unit], both, preferred_element_type=F32)
            value = product if value is None else value + product
        if final:
            value = value + jnp.dot(low_rows[unit], tables[...], preferred_element_type=F32)
            value = value + start_ref[unit]
            half = value.shape[1] // 2
            gate, up = value[:, :half], value[:, half:]
            out_ref[unit] = (gate / (1.0 + jnp.exp(-gate)) * up).astype(BF16)
        else:
            out_ref[unit] = value
        return carry

    for g in range(units // block):
        for copy in copies[g * 2 * quarters : (g + 1) * 2 * quarters]:
            copy.wait()
        lax.fori_loop(g * block, (g + 1) * block, one, 0, unroll=block)


def expand(sources, layout, first, scalars, pick, gate_weight, up_weight, final=None):
    units, width, share = gate_weight.shape
    wide = width // 4
    quarters = len(sources) // len(layout)
    rows = GROUP * SLOT
    args = list(sources) + [pick, gate_weight, up_weight]
    scratch = [
        pltpu.VMEM((quarters, units, rows, wide), BF16),
        pltpu.VMEM((quarters, 2, units, wide, share), BF16),
        pltpu.SemaphoreType.DMA((units, quarters, 2)),
    ]
    if final is None:
        out_shape = jax.ShapeDtypeStruct((units, rows, 2 * share), F32)
    else:
        args += list(final)
        out_shape = jax.ShapeDtypeStruct((units, rows, share), BF16)
        scratch += [pltpu.VMEM((units, rows, rows), BF16), pltpu.VMEM((rows, 2 * share), BF16)]
    count = len(sources) + 1
    vmem = pl.BlockSpec(memory_space=pltpu.VMEM)
    hbm = pl.BlockSpec(memory_space=pl.ANY)
    return pl.pallas_call(
        functools.partial(expand_kernel, units, quarters, first, layout, final is not None),
        in_specs=[pl.BlockSpec(memory_space=pltpu.SMEM)] + [vmem] * count + [hbm, hbm] + [vmem] * (len(args) - count - 2),
        out_specs=vmem,
        scratch_shapes=scratch,
        out_shape=out_shape,
        compiler_params=params(EXPAND_BYTES),
        cost_estimate=COST,
    )(scalars, *args)


def contract_kernel(units, jobs, parts, scalar_ref, down_hbm, hidden_ref, place_ref, gain_ref, *refs):
    outs, (table, down_ref, done) = refs[:-3], refs[-3:]
    wide = table.shape[2]
    copies = []
    for n, (part, q) in enumerate(jobs):
        at = pl.ds(pl.multiple_of(((scalar_ref[0] ^ q) * parts + part) * wide, wide), wide)
        copies.append(pltpu.make_async_copy(down_hbm.at[:, at, :], down_ref.at[n], done.at[n]))
        copies[n].start()
    for n in range(len(jobs)):
        copies[n].wait()

        def one(unit, carry, n=n):
            rows = nt_dot(hidden_ref[unit], down_ref[n, unit])
            gain = jnp.concatenate([gain_ref[unit]] * (wide // 128), axis=1)
            spot = pl.ds(pl.multiple_of(unit * SLOT, SLOT), SLOT)
            table[:, spot, :] = (rows * gain).astype(BF16).reshape(GROUP, SLOT, wide)
            return carry

        lax.fori_loop(0, units, one, 0, unroll=min(units, UNROLL))
        for r in range(GROUP):
            sums = jnp.dot(place_ref[r], table[r], preferred_element_type=F32)
            outs[n][r] = sums.astype(outs[n].dtype)


def contract(hidden, down_weight, place, gain, scalars, jobs, parts):
    units, width, share = down_weight.shape
    tokens = place.shape[1]
    wide = width // 4 // parts
    vmem = pl.BlockSpec(memory_space=pltpu.VMEM)
    return pl.pallas_call(
        functools.partial(contract_kernel, units, jobs, parts),
        in_specs=[pl.BlockSpec(memory_space=pltpu.SMEM), pl.BlockSpec(memory_space=pl.ANY)] + [vmem] * 3,
        out_specs=[vmem] * len(jobs),
        scratch_shapes=[
            pltpu.VMEM((GROUP, units * SLOT, wide), BF16),
            pltpu.VMEM((len(jobs), units, wide, share), BF16),
            pltpu.SemaphoreType.DMA((len(jobs),)),
        ],
        out_shape=[jax.ShapeDtypeStruct((GROUP, tokens, wide), BF16 if q % 2 else F32) for _, q in jobs],
        compiler_params=params(EXPAND_BYTES),
        cost_estimate=COST,
    )(scalars, down_weight, hidden, place, gain)


def xor_move(value, axis, bits):
    size = lax.axis_size(axis)
    return lax.ppermute(value, axis, [(i, i ^ bits) for i in range(size)])


def select_adapters(request_adapter, rows_local, row_index):
    wanted = request_adapter[:, None] * DOUBLE_RANK + jnp.arange(DOUBLE_RANK)[None, :]
    held = row_index * rows_local + jnp.arange(rows_local)
    return (wanted.reshape(-1)[:, None] == held[None, :]).astype(BF16)


def widen_tables(tables):
    is_gate = (jnp.arange(DOUBLE_RANK) < ADAPTER_RANK)[None, :, None]
    zero = jnp.zeros_like(tables)
    return jnp.concatenate([jnp.where(is_gate, tables, zero), jnp.where(is_gate, zero, tables)], axis=2)


def meta_of(token_experts, router_weight):
    left = router_weight.T
    terms = []
    for _ in range(3):
        term = lax.reduce_precision(left, 8, 7)
        terms.append(term.astype(BF16))
        left = left - term
    return jnp.concatenate([token_experts.T.astype(BF16)] + terms, axis=1)


def end_along_z(here):
    last = here[0]
    for k in (1, 2, 3):
        last = last + xor_move(here[k].astype(BF16), "dp", 2 * k).astype(F32)
    return last.astype(BF16)


def near_device(
    tokens,
    lengths,
    request_adapter,
    token_experts,
    router_weight,
    gate_weight,
    up_weight,
    down_weight,
    adapter_input_maps,
    adapter_output_maps,
):
    width = tokens.shape[1]
    units = gate_weight.shape[0]
    dp_count = lax.axis_size("dp")
    tp_count = lax.axis_size("tensor")
    i = lax.axis_index("dp")
    j = lax.axis_index("tensor")
    experts_all = units * dp_count // 2
    quarter = width // tp_count
    rel = i ^ jnp.array(ORDER, jnp.int32)
    tok_rows = tokens.shape[0]
    own = lax.dynamic_slice_in_dim(tokens, j * quarter, quarter, 1)

    block = jnp.concatenate([own, meta_of(token_experts, router_weight)], axis=0)
    ahead = [xor_move(block, "dp", n) for n in (1, 2, 4, 6)]
    layout = ((0,), (4, 1, 2, 3), (5, 6, 7))

    natural = i ^ jnp.array(HALVING, jnp.int32)
    adapters = jnp.sum(
        jnp.where(natural[:, None] == jnp.arange(dp_count)[None, :], request_adapter[None, :], 0), axis=1
    )
    columns = nt_dot(select_adapters(adapters, adapter_input_maps.shape[1], i), adapter_input_maps)
    columns = columns.astype(BF16)

    halves = adapter_output_maps.reshape(adapter_output_maps.shape[0], -1)
    tables = jnp.dot(
        select_adapters(request_adapter, halves.shape[0], i), halves, preferred_element_type=F32
    ).astype(BF16)
    share = halves.shape[1] // 2
    upper = i >= dp_count // 2
    first_expert = (i * units) % experts_all
    is_rel = rel[:, None] == jnp.arange(dp_count)[None, :]
    lengths_rel = jnp.sum(jnp.where(is_rel, lengths[None, :], 0), axis=1)
    slot_scalars = jnp.concatenate([first_expert[None], lengths_rel]).astype(jnp.int32)
    scalars = jnp.concatenate([j[None], rel]).astype(jnp.int32)
    strips = quarter // share

    def strip(rows):
        return [rows[:, n * share : (n + 1) * share] for n in range(rows.shape[1] // share)]

    def halve(columns, given, bits):
        kept = columns.shape[0] // 2
        got = xor_move(jnp.concatenate(strip(columns[kept:]) + given, axis=0), "dp", bits)
        more = jnp.concatenate([got[n * kept : (n + 1) * kept] for n in range(strips)], axis=1)
        got = got[strips * kept :]
        size = given[0].shape[0]
        return columns[:kept] + more, [got[n * size : (n + 1) * size] for n in range(len(given))]

    tables = strip(tables)
    columns, came = halve(columns, tables, 1)
    tables = [t + c for t, c in zip(tables, came, strict=True)]

    ahead, columns, tables = lax.optimization_barrier((ahead, columns, tables))
    behind = xor_move(jnp.stack(ahead[1:]), "dp", 1)
    ahead = jnp.stack(ahead)
    side_ahead = xor_move(ahead, "tensor", 2)
    core_ahead = xor_move(ahead, "tensor", 1)
    columns, came = halve(columns, tables, 2)
    tables = [t + c for t, c in zip(tables, came, strict=True)]
    mine, other = jnp.where(upper, tables[1], tables[0]), jnp.where(upper, tables[0], tables[1])
    columns, came = halve(columns, [other], 4)
    tables = mine + came[0]
    low = nt_dot(columns, own)
    low = low + xor_move(low, "tensor", 1)

    behind, low, tables, side_ahead = lax.optimization_barrier((behind, low, tables, side_ahead))
    low = low + xor_move(low, "tensor", 2)
    side_behind = xor_move(behind, "tensor", 2)
    core_behind = xor_move(behind, "tensor", 1)
    low = low.astype(BF16)[None]
    for bits in (4, 2):
        low = jnp.concatenate([low, xor_move(low, "dp", bits)], axis=0)
    both_ahead = xor_move(side_ahead, "tensor", 1)
    tables = widen_tables(tables.reshape(dp_count, DOUBLE_RANK, share))

    routes = block.shape[0] - tok_rows
    meta_specs = [
        pl.BlockSpec((n, routes, quarter), lambda *_: (0, tok_rows // routes, 0)) for n in (1, 3, 1, 3)
    ]
    meta_specs[2] = pl.BlockSpec((1, routes, quarter), lambda *_: (0, tok_rows // routes, 0))
    meta_specs[1] = pl.BlockSpec((3, routes, quarter), lambda *_: (0, tok_rows // routes, 0))
    pick, place, gain = make_slots(
        [block[None], ahead[1:], ahead[:1], behind], meta_specs, tok_rows, slot_scalars, units
    )

    def sources(*pairs):
        return [x for pair in pairs for x in (tokens,) + pair]

    start = expand(
        sources((ahead, behind), (core_ahead, core_behind)), layout, 0, scalars, pick, gate_weight, up_weight
    )
    start, side_behind, low = lax.optimization_barrier((start, side_behind, low))
    low = jnp.concatenate([low, xor_move(low, "dp", 1)], axis=0)
    low = jnp.stack([low[GATHERED.index(n)] for n in ORDER])
    both_behind = xor_move(side_behind, "tensor", 1)
    hidden = expand(
        sources((side_ahead, side_behind), (both_ahead, both_behind)),
        layout,
        2,
        scalars,
        pick,
        gate_weight,
        up_weight,
        (start, low, tables),
    )

    def core_sum(send, keep):
        return keep + xor_move(send, "tensor", 1).astype(F32)

    early = contract(hidden, down_weight, place, gain, scalars, ((1, 3), (1, 2), (0, 3), (0, 2)), 2)
    there = core_sum(*early[2:]).astype(BF16)
    second_there = core_sum(*early[:2])
    there, second_there, hidden = lax.optimization_barrier((there, second_there, hidden))
    above = xor_move(there[4:], "tensor", 2)
    below = xor_move(there[:4], "tensor", 2)
    across = xor_move(second_there[4:].astype(BF16), "dp", 1)

    late = contract(hidden, down_weight, place, gain, scalars, ((0, 1), (0, 0), (1, 1), (1, 0)), 2)
    late, above, across = lax.optimization_barrier((late, above, across))
    second_there = xor_move((second_there[:4] + across.astype(F32)).astype(BF16), "tensor", 2)
    here = core_sum(*late[:2])
    given = (here[4:] + above.astype(F32)).astype(BF16)
    here = here[:4] + below.astype(F32) + xor_move(given, "dp", 1).astype(F32)
    first = end_along_z(here)
    here = core_sum(*late[2:])
    here = here[:4] + xor_move(here[4:].astype(BF16), "dp", 1).astype(F32) + second_there.astype(F32)
    second = end_along_z(here)
    return jnp.concatenate([first, second], axis=1)


def any_device(
    tokens,
    lengths,
    request_adapter,
    token_experts,
    router_weight,
    gate_weight,
    up_weight,
    down_weight,
    adapter_input_maps,
    adapter_output_maps,
):
    tok_rows, width = tokens.shape
    units = gate_weight.shape[0]
    dp_count = lax.axis_size("dp")
    tp_count = lax.axis_size("tensor")
    i = lax.axis_index("dp")
    j = lax.axis_index("tensor")
    experts_all = units * dp_count // 2
    quarter = width // tp_count
    meta = lax.all_gather(meta_of(token_experts, router_weight), "dp", axis=0)
    rows = lax.all_gather(tokens, "dp", axis=0)
    maps = lax.all_gather(adapter_input_maps, "dp", axis=1, tiled=True)
    adapter = jnp.sum(jnp.where(jnp.arange(dp_count) == i, request_adapter, 0))
    columns = nt_dot(select_adapters(adapter[None], maps.shape[1], 0), maps).astype(BF16)
    x_part = lax.dynamic_slice_in_dim(tokens, j * quarter, quarter, 1)
    low = lax.psum(nt_dot(columns, x_part), "tensor").astype(BF16)
    low = lax.all_gather(low, "dp", axis=0)
    every = lax.all_gather(adapter_output_maps, "dp", axis=0, tiled=True)
    half = jnp.where(i * units >= experts_all, every[:, 1], every[:, 0])
    tables = jnp.dot(
        select_adapters(request_adapter, half.shape[0], 0), half, preferred_element_type=F32
    ).astype(BF16)
    tables = widen_tables(tables.reshape(dp_count, DOUBLE_RANK, half.shape[1]))
    first_expert = (i * units) % experts_all
    natural = jnp.concatenate([j[None], jnp.arange(GROUP)]).astype(jnp.int32)

    def one_group(group):
        meta_g, rows_g, low_g, tables_g, lengths_g = group
        pick, place, gain = make_slots(
            [meta_g],
            [full_spec(meta_g.shape)],
            tok_rows,
            jnp.concatenate([first_expert[None], lengths_g]).astype(jnp.int32),
            units,
        )
        layout = (tuple(range(GROUP)),)

        start = expand([rows_g] * 2, layout, 0, natural, pick, gate_weight, up_weight)
        hidden = expand(
            [rows_g] * 2, layout, 2, natural, pick, gate_weight, up_weight, (start, low_g, tables_g)
        )
        jobs = tuple((0, q) for q in range(4))
        sums = contract(hidden, down_weight, place, gain, natural, jobs, 1)
        return tuple(a.astype(BF16) for a in sums)

    groups = dp_count // GROUP
    grouped = [
        a.reshape((groups, GROUP) + a.shape[1:]) for a in (meta, rows, low, tables, lengths)
    ]
    sums = lax.map(one_group, tuple(grouped))
    sums = [a.reshape(dp_count * tok_rows, quarter) for a in sums]
    here = sums[0].astype(F32)
    for q in range(1, 4):
        here = here + xor_move(sums[q], "tensor", q).astype(F32)
    return lax.psum_scatter(here, "dp", scatter_dimension=0, tiled=True).astype(BF16)


def solution(mesh):
    near = mesh.shape["dp"] == 8 and mesh.shape["tensor"] == 4
    in_specs = (
        P("dp", None),
        P(),
        P(),
        P("dp", None),
        P("dp", None),
        P("dp", None, "tensor"),
        P("dp", None, "tensor"),
        P("dp", None, "tensor"),
        P("tensor", "dp"),
        P("dp", None, "tensor"),
    )
    return jax.shard_map(
        near_device if near else any_device,
        mesh=mesh,
        in_specs=in_specs,
        out_specs=P("dp", "tensor"),
        check_vma=False,
    )
```

```python
import functools

import jax
import jax.numpy as jnp
from jax import lax
from jax.experimental import pallas as pl
from jax.experimental.pallas import tpu as pltpu
from jax.sharding import PartitionSpec as P

ADAPTER_RANK = 16
DOUBLE_RANK = 2 * ADAPTER_RANK
CAP = 28
SLOT = 32
GROUP = 8
BF16 = jnp.bfloat16
F32 = jnp.float32
VMEM_BYTES = 12 * 1024 * 1024
EXPAND_BYTES = 42 * 1024 * 1024
UNROLL = 16
COST = pl.CostEstimate(flops=1_000_000, bytes_accessed=1_000, transcendentals=0)
ORDER = (0, 2, 4, 6, 1, 3, 5, 7)
HALVING = (0, 4, 2, 6, 1, 5, 3, 7)
GATHERED = (0, 4, 2, 6, 1, 5, 3, 7)


def params(size=VMEM_BYTES):
    return pltpu.CompilerParams(vmem_limit_bytes=size)


def full_spec(shape):
    return pl.BlockSpec(shape, lambda *_: (0,) * len(shape))


def nt_dot(a, b):
    return lax.dot_general(a, b, (((1,), (1,)), ((), ())), preferred_element_type=F32)


def slots_kernel(units, scalar_ref, *refs):
    metas, (pick_ref, place_ref, gain_ref) = refs[:-3], refs[-3:]
    metas = [m.at[n] for m in metas for n in range(m.shape[0])]
    rows = max(units, 8)
    topk = metas[0].shape[0]
    tokens = metas[0].shape[1] // 4
    first = scalar_ref[0]
    expert = (lax.broadcasted_iota(jnp.int32, (rows, tokens), 0) + first).astype(F32)
    token = lax.broadcasted_iota(jnp.int32, (rows, tokens), 1)
    slot = lax.broadcasted_iota(jnp.int32, (units, SLOT, tokens), 1).astype(F32)
    before = (
        lax.broadcasted_iota(jnp.int32, (tokens, tokens), 0)
        < lax.broadcasted_iota(jnp.int32, (tokens, tokens), 1)
    ).astype(BF16)
    for r in range(GROUP):
        live = token < scalar_ref[1 + r]
        meta = metas[r][...].astype(F32)
        ids = meta[:, :tokens]
        weights = meta[:, tokens : 2 * tokens] + meta[:, 2 * tokens : 3 * tokens] + meta[:, 3 * tokens :]
        hit = jnp.zeros((rows, tokens), F32)
        gain = jnp.zeros((rows, tokens), F32)
        for k in range(topk):
            same = jnp.broadcast_to(ids[k : k + 1], (rows, tokens)) == expert
            hit = hit + jnp.where(same, 1.0, 0.0)
            gain = gain + jnp.where(same, jnp.broadcast_to(weights[k : k + 1], (rows, tokens)), 0.0)
        hit = jnp.where(live, hit, 0.0)
        position = jnp.dot(hit.astype(BF16), before, preferred_element_type=F32)
        position = jnp.where(hit > 0.5, position, -1.0)[:units]
        pick = jnp.where(jnp.broadcast_to(position[:, None, :], slot.shape) == slot, 1.0, 0.0)
        gains = jnp.sum(pick * gain[:units][:, None, :], axis=2, keepdims=True)
        gain_ref[:, r * SLOT : (r + 1) * SLOT, :] = jnp.broadcast_to(gains, (units, SLOT, 128))
        pick = pick.reshape(units * SLOT, tokens)
        pick_ref[r] = pick.astype(BF16)
        place_ref[r] = pick.T.astype(BF16)


def make_slots(metas, specs, tokens, scalars, units):
    slots = units * SLOT
    return pl.pallas_call(
        functools.partial(slots_kernel, units),
        grid_spec=pltpu.PrefetchScalarGridSpec(
            num_scalar_prefetch=1,
            grid=(1,),
            in_specs=specs,
            out_specs=[
                full_spec((GROUP, slots, tokens)),
                full_spec((GROUP, tokens, slots)),
                full_spec((units, GROUP * SLOT, 128)),
            ],
        ),
        out_shape=[
            jax.ShapeDtypeStruct((GROUP, slots, tokens), BF16),
            jax.ShapeDtypeStruct((GROUP, tokens, slots), BF16),
            jax.ShapeDtypeStruct((units, GROUP * SLOT, 128), F32),
        ],
        compiler_params=params(),
        cost_estimate=COST,
    )(scalars, *metas)


def expand_kernel(units, quarters, first, layout, final, scalar_ref, *refs):
    count = len(layout)
    groups, refs = refs[: quarters * count], refs[quarters * count :]
    if final:
        pick_ref, gate_hbm, up_hbm, start_ref, low_ref, table_ref = refs[:6]
        out_ref, gathered, both_ref, done, low_rows, tables = refs[6:]
    else:
        pick_ref, gate_hbm, up_hbm, out_ref, gathered, both_ref, done = refs
    tokens, wide = pick_ref.shape[2], gathered.shape[3]
    places = [slice(r * SLOT, (r + 1) * SLOT) for r in range(GROUP)]
    at = [
        pl.ds(pl.multiple_of((scalar_ref[0] ^ (first + turn)) * wide, wide), wide)
        for turn in range(quarters)
    ]

    block = min(units, 4)
    copies = []
    for g in range(units // block):
        part = pl.ds(g * block, block)
        for turn in range(quarters):
            for n, weight in enumerate((gate_hbm, up_hbm)):
                copy = pltpu.make_async_copy(
                    weight.at[part, at[turn], :], both_ref.at[turn, n, part], done.at[g, turn, n]
                )
                copy.start()
                copies.append(copy)

    def scatter(target, r, rows):
        target[:, places[r], :] = rows.astype(BF16).reshape(units, SLOT, rows.shape[1])

    for turn in range(quarters):
        for source, spots in zip(groups[turn * count : (turn + 1) * count], layout, strict=True):
            for n, r in enumerate(spots):
                if len(source.shape) == 2:
                    block_rows = source[:, at[turn]]
                elif source.shape[2] == wide:
                    block_rows = source[n, :tokens, :]
                else:
                    block_rows = source[n, :, at[turn]]
                scatter(gathered.at[turn], r, jnp.dot(pick_ref[r], block_rows, preferred_element_type=F32))
    if final:
        zero = jnp.zeros((SLOT, tokens), BF16)
        for r in range(GROUP):
            spread = jnp.concatenate([zero] * r + [low_ref[r]] + [zero] * (GROUP - 1 - r), axis=0)
            scatter(low_rows, r, nt_dot(pick_ref[r], spread))
            tables[places[r], :] = table_ref[scalar_ref[1 + r]]

    def one(unit, carry):
        value = None
        for turn in range(quarters):
            both = jnp.concatenate([both_ref[turn, 0, unit], both_ref[turn, 1, unit]], axis=1)
            product = jnp.dot(gathered[turn, unit], both, preferred_element_type=F32)
            value = product if value is None else value + product
        if final:
            value = value + jnp.dot(low_rows[unit], tables[...], preferred_element_type=F32)
            value = value + start_ref[unit]
            half = value.shape[1] // 2
            gate, up = value[:, :half], value[:, half:]
            out_ref[unit] = (gate / (1.0 + jnp.exp(-gate)) * up).astype(BF16)
        else:
            out_ref[unit] = value
        return carry

    for g in range(units // block):
        for copy in copies[g * 2 * quarters : (g + 1) * 2 * quarters]:
            copy.wait()
        lax.fori_loop(g * block, (g + 1) * block, one, 0, unroll=block)


def expand(sources, layout, first, scalars, pick, gate_weight, up_weight, final=None):
    units, width, share = gate_weight.shape
    wide = width // 4
    quarters = len(sources) // len(layout)
    rows = GROUP * SLOT
    args = list(sources) + [pick, gate_weight, up_weight]
    scratch = [
        pltpu.VMEM((quarters, units, rows, wide), BF16),
        pltpu.VMEM((quarters, 2, units, wide, share), BF16),
        pltpu.SemaphoreType.DMA((units, quarters, 2)),
    ]
    if final is None:
        out_shape = jax.ShapeDtypeStruct((units, rows, 2 * share), F32)
    else:
        args += list(final)
        out_shape = jax.ShapeDtypeStruct((units, rows, share), BF16)
        scratch += [pltpu.VMEM((units, rows, rows), BF16), pltpu.VMEM((rows, 2 * share), BF16)]
    count = len(sources) + 1
    vmem = pl.BlockSpec(memory_space=pltpu.VMEM)
    hbm = pl.BlockSpec(memory_space=pl.ANY)
    return pl.pallas_call(
        functools.partial(expand_kernel, units, quarters, first, layout, final is not None),
        in_specs=[pl.BlockSpec(memory_space=pltpu.SMEM)] + [vmem] * count + [hbm, hbm] + [vmem] * (len(args) - count - 2),
        out_specs=vmem,
        scratch_shapes=scratch,
        out_shape=out_shape,
        compiler_params=params(EXPAND_BYTES),
        cost_estimate=COST,
    )(scalars, *args)


def contract_kernel(units, jobs, parts, scalar_ref, down_hbm, hidden_ref, place_ref, gain_ref, *refs):
    outs, (table, down_ref, done) = refs[:-3], refs[-3:]
    wide = table.shape[2]
    copies = []
    for n, (part, q) in enumerate(jobs):
        at = pl.ds(pl.multiple_of(((scalar_ref[0] ^ q) * parts + part) * wide, wide), wide)
        copies.append(pltpu.make_async_copy(down_hbm.at[:, at, :], down_ref.at[n], done.at[n]))
        copies[n].start()
    for n in range(len(jobs)):
        copies[n].wait()

        def one(unit, carry, n=n):
            rows = nt_dot(hidden_ref[unit], down_ref[n, unit])
            gain = jnp.concatenate([gain_ref[unit]] * (wide // 128), axis=1)
            spot = pl.ds(pl.multiple_of(unit * SLOT, SLOT), SLOT)
            table[:, spot, :] = (rows * gain).astype(BF16).reshape(GROUP, SLOT, wide)
            return carry

        lax.fori_loop(0, units, one, 0, unroll=min(units, UNROLL))
        for r in range(GROUP):
            sums = jnp.dot(place_ref[r], table[r], preferred_element_type=F32)
            outs[n][r] = sums.astype(outs[n].dtype)


def contract(hidden, down_weight, place, gain, scalars, jobs, parts):
    units, width, share = down_weight.shape
    tokens = place.shape[1]
    wide = width // 4 // parts
    vmem = pl.BlockSpec(memory_space=pltpu.VMEM)
    return pl.pallas_call(
        functools.partial(contract_kernel, units, jobs, parts),
        in_specs=[pl.BlockSpec(memory_space=pltpu.SMEM), pl.BlockSpec(memory_space=pl.ANY)] + [vmem] * 3,
        out_specs=[vmem] * len(jobs),
        scratch_shapes=[
            pltpu.VMEM((GROUP, units * SLOT, wide), BF16),
            pltpu.VMEM((len(jobs), units, wide, share), BF16),
            pltpu.SemaphoreType.DMA((len(jobs),)),
        ],
        out_shape=[jax.ShapeDtypeStruct((GROUP, tokens, wide), BF16 if q % 2 else F32) for _, q in jobs],
        compiler_params=params(EXPAND_BYTES),
        cost_estimate=COST,
    )(scalars, down_weight, hidden, place, gain)


def xor_move(value, axis, bits):
    size = lax.axis_size(axis)
    return lax.ppermute(value, axis, [(i, i ^ bits) for i in range(size)])


def select_adapters(request_adapter, rows_local, row_index):
    wanted = request_adapter[:, None] * DOUBLE_RANK + jnp.arange(DOUBLE_RANK)[None, :]
    held = row_index * rows_local + jnp.arange(rows_local)
    return (wanted.reshape(-1)[:, None] == held[None, :]).astype(BF16)


def widen_tables(tables):
    is_gate = (jnp.arange(DOUBLE_RANK) < ADAPTER_RANK)[None, :, None]
    zero = jnp.zeros_like(tables)
    return jnp.concatenate([jnp.where(is_gate, tables, zero), jnp.where(is_gate, zero, tables)], axis=2)


def meta_of(token_experts, router_weight):
    left = router_weight.T
    terms = []
    for _ in range(3):
        term = lax.reduce_precision(left, 8, 7)
        terms.append(term.astype(BF16))
        left = left - term
    return jnp.concatenate([token_experts.T.astype(BF16)] + terms, axis=1)


def end_along_z(here):
    last = here[0]
    for k in (1, 2, 3):
        last = last + xor_move(here[k].astype(BF16), "dp", 2 * k).astype(F32)
    return last.astype(BF16)


def near_device(
    tokens,
    lengths,
    request_adapter,
    token_experts,
    router_weight,
    gate_weight,
    up_weight,
    down_weight,
    adapter_input_maps,
    adapter_output_maps,
):
    width = tokens.shape[1]
    units = gate_weight.shape[0]
    dp_count = lax.axis_size("dp")
    tp_count = lax.axis_size("tensor")
    i = lax.axis_index("dp")
    j = lax.axis_index("tensor")
    experts_all = units * dp_count // 2
    quarter = width // tp_count
    rel = i ^ jnp.array(ORDER, jnp.int32)
    tok_rows = tokens.shape[0]
    own = lax.dynamic_slice_in_dim(tokens, j * quarter, quarter, 1)

    block = jnp.concatenate([own, meta_of(token_experts, router_weight)], axis=0)
    ahead = [xor_move(block, "dp", n) for n in (1, 2, 4, 6)]
    layout = ((0,), (4, 1, 2, 3), (5, 6, 7))

    natural = i ^ jnp.array(HALVING, jnp.int32)
    adapters = jnp.sum(
        jnp.where(natural[:, None] == jnp.arange(dp_count)[None, :], request_adapter[None, :], 0), axis=1
    )
    columns = nt_dot(select_adapters(adapters, adapter_input_maps.shape[1], i), adapter_input_maps)
    columns = columns.astype(BF16)

    halves = adapter_output_maps.reshape(adapter_output_maps.shape[0], -1)
    tables = jnp.dot(
        select_adapters(request_adapter, halves.shape[0], i), halves, preferred_element_type=F32
    ).astype(BF16)
    share = halves.shape[1] // 2
    upper = i >= dp_count // 2
    first_expert = (i * units) % experts_all
    is_rel = rel[:, None] == jnp.arange(dp_count)[None, :]
    lengths_rel = jnp.sum(jnp.where(is_rel, lengths[None, :], 0), axis=1)
    slot_scalars = jnp.concatenate([first_expert[None], lengths_rel]).astype(jnp.int32)
    scalars = jnp.concatenate([j[None], rel]).astype(jnp.int32)
    strips = quarter // share

    def strip(rows):
        return [rows[:, n * share : (n + 1) * share] for n in range(rows.shape[1] // share)]

    def halve(columns, given, bits):
        kept = columns.shape[0] // 2
        got = xor_move(jnp.concatenate(strip(columns[kept:]) + given, axis=0), "dp", bits)
        more = jnp.concatenate([got[n * kept : (n + 1) * kept] for n in range(strips)], axis=1)
        got = got[strips * kept :]
        size = given[0].shape[0]
        return columns[:kept] + more, [got[n * size : (n + 1) * size] for n in range(len(given))]

    tables = strip(tables)
    columns, came = halve(columns, tables, 1)
    tables = [t + c for t, c in zip(tables, came, strict=True)]

    ahead, columns, tables = lax.optimization_barrier((ahead, columns, tables))
    behind = xor_move(jnp.stack(ahead[1:]), "dp", 1)
    ahead = jnp.stack(ahead)
    side_ahead = xor_move(ahead, "tensor", 2)
    core_ahead = xor_move(ahead, "tensor", 1)
    columns, came = halve(columns, tables, 2)
    tables = [t + c for t, c in zip(tables, came, strict=True)]
    mine, other = jnp.where(upper, tables[1], tables[0]), jnp.where(upper, tables[0], tables[1])
    columns, came = halve(columns, [other], 4)
    tables = mine + came[0]
    low = nt_dot(columns, own)
    low = low + xor_move(low, "tensor", 1)

    behind, low, tables, side_ahead = lax.optimization_barrier((behind, low, tables, side_ahead))
    low = low + xor_move(low, "tensor", 2)
    side_behind = xor_move(behind, "tensor", 2)
    core_behind = xor_move(behind, "tensor", 1)
    low = low.astype(BF16)[None]
    for bits in (4, 2):
        low = jnp.concatenate([low, xor_move(low, "dp", bits)], axis=0)
    both_ahead = xor_move(side_ahead, "tensor", 1)
    tables = widen_tables(tables.reshape(dp_count, DOUBLE_RANK, share))

    routes = block.shape[0] - tok_rows
    meta_specs = [
        pl.BlockSpec((n, routes, quarter), lambda *_: (0, tok_rows // routes, 0)) for n in (1, 3, 1, 3)
    ]
    meta_specs[2] = pl.BlockSpec((1, routes, quarter), lambda *_: (0, tok_rows // routes, 0))
    meta_specs[1] = pl.BlockSpec((3, routes, quarter), lambda *_: (0, tok_rows // routes, 0))
    pick, place, gain = make_slots(
        [block[None], ahead[1:], ahead[:1], behind], meta_specs, tok_rows, slot_scalars, units
    )

    def sources(*pairs):
        return [x for pair in pairs for x in (tokens,) + pair]

    start = expand(
        sources((ahead, behind), (core_ahead, core_behind)), layout, 0, scalars, pick, gate_weight, up_weight
    )
    start, side_behind, low = lax.optimization_barrier((start, side_behind, low))
    low = jnp.concatenate([low, xor_move(low, "dp", 1)], axis=0)
    low = jnp.stack([low[GATHERED.index(n)] for n in ORDER])
    both_behind = xor_move(side_behind, "tensor", 1)
    hidden = expand(
        sources((side_ahead, side_behind), (both_ahead, both_behind)),
        layout,
        2,
        scalars,
        pick,
        gate_weight,
        up_weight,
        (start, low, tables),
    )

    def core_sum(send, keep):
        return keep + xor_move(send, "tensor", 1).astype(F32)

    early = contract(hidden, down_weight, place, gain, scalars, ((1, 3), (1, 2), (0, 3), (0, 2)), 2)
    there = core_sum(*early[2:]).astype(BF16)
    second_there = core_sum(*early[:2])
    there, second_there, hidden = lax.optimization_barrier((there, second_there, hidden))
    above = xor_move(there[4:], "tensor", 2)
    below = xor_move(there[:4], "tensor", 2)
    across = xor_move(second_there[4:].astype(BF16), "dp", 1)

    late = contract(hidden, down_weight, place, gain, scalars, ((0, 1), (0, 0), (1, 1), (1, 0)), 2)
    late, above, across = lax.optimization_barrier((late, above, across))
    second_there = xor_move((second_there[:4] + across.astype(F32)).astype(BF16), "tensor", 2)
    here = core_sum(*late[:2])
    given = (here[4:] + above.astype(F32)).astype(BF16)
    here = here[:4] + below.astype(F32) + xor_move(given, "dp", 1).astype(F32)
    first = end_along_z(here)
    here = core_sum(*late[2:])
    here = here[:4] + xor_move(here[4:].astype(BF16), "dp", 1).astype(F32) + second_there.astype(F32)
    second = end_along_z(here)
    return jnp.concatenate([first, second], axis=1)


def any_device(
    tokens,
    lengths,
    request_adapter,
    token_experts,
    router_weight,
    gate_weight,
    up_weight,
    down_weight,
    adapter_input_maps,
    adapter_output_maps,
):
    tok_rows, width = tokens.shape
    units = gate_weight.shape[0]
    dp_count = lax.axis_size("dp")
    tp_count = lax.axis_size("tensor")
    i = lax.axis_index("dp")
    j = lax.axis_index("tensor")
    experts_all = units * dp_count // 2
    quarter = width // tp_count
    meta = lax.all_gather(meta_of(token_experts, router_weight), "dp", axis=0)
    rows = lax.all_gather(tokens, "dp", axis=0)
    maps = lax.all_gather(adapter_input_maps, "dp", axis=1, tiled=True)
    adapter = jnp.sum(jnp.where(jnp.arange(dp_count) == i, request_adapter, 0))
    columns = nt_dot(select_adapters(adapter[None], maps.shape[1], 0), maps).astype(BF16)
    x_part = lax.dynamic_slice_in_dim(tokens, j * quarter, quarter, 1)
    low = lax.psum(nt_dot(columns, x_part), "tensor").astype(BF16)
    low = lax.all_gather(low, "dp", axis=0)
    every = lax.all_gather(adapter_output_maps, "dp", axis=0, tiled=True)
    half = jnp.where(i * units >= experts_all, every[:, 1], every[:, 0])
    tables = jnp.dot(
        select_adapters(request_adapter, half.shape[0], 0), half, preferred_element_type=F32
    ).astype(BF16)
    tables = widen_tables(tables.reshape(dp_count, DOUBLE_RANK, half.shape[1]))
    first_expert = (i * units) % experts_all
    natural = jnp.concatenate([j[None], jnp.arange(GROUP)]).astype(jnp.int32)

    def one_group(group):
        meta_g, rows_g, low_g, tables_g, lengths_g = group
        pick, place, gain = make_slots(
            [meta_g],
            [full_spec(meta_g.shape)],
            tok_rows,
            jnp.concatenate([first_expert[None], lengths_g]).astype(jnp.int32),
            units,
        )
        layout = (tuple(range(GROUP)),)

        start = expand([rows_g] * 2, layout, 0, natural, pick, gate_weight, up_weight)
        hidden = expand(
            [rows_g] * 2, layout, 2, natural, pick, gate_weight, up_weight, (start, low_g, tables_g)
        )
        jobs = tuple((0, q) for q in range(4))
        sums = contract(hidden, down_weight, place, gain, natural, jobs, 1)
        return tuple(a.astype(BF16) for a in sums)

    groups = dp_count // GROUP
    grouped = [
        a.reshape((groups, GROUP) + a.shape[1:]) for a in (meta, rows, low, tables, lengths)
    ]
    sums = lax.map(one_group, tuple(grouped))
    sums = [a.reshape(dp_count * tok_rows, quarter) for a in sums]
    here = sums[0].astype(F32)
    for q in range(1, 4):
        here = here + xor_move(sums[q], "tensor", q).astype(F32)
    return lax.psum_scatter(here, "dp", scatter_dimension=0, tiled=True).astype(BF16)


def solution(mesh):
    near = mesh.shape["dp"] == 8 and mesh.shape["tensor"] == 4
    in_specs = (
        P("dp", None),
        P(),
        P(),
        P("dp", None),
        P("dp", None),
        P("dp", None, "tensor"),
        P("dp", None, "tensor"),
        P("dp", None, "tensor"),
        P("tensor", "dp"),
        P("dp", None, "tensor"),
    )
    return jax.shard_map(
        near_device if near else any_device,
        mesh=mesh,
        in_specs=in_specs,
        out_specs=P("dp", "tensor"),
        check_vma=False,
    )
```

```python
import functools

import jax
import jax.numpy as jnp
from jax import lax
from jax.experimental import pallas as pl
from jax.experimental.pallas import tpu as pltpu
from jax.sharding import PartitionSpec as P

ADAPTER_RANK = 16
DOUBLE_RANK = 2 * ADAPTER_RANK
CAP = 28
SLOT = 32
GROUP = 8
BF16 = jnp.bfloat16
F32 = jnp.float32
VMEM_BYTES = 12 * 1024 * 1024
EXPAND_BYTES = 42 * 1024 * 1024
UNROLL = 16
COST = pl.CostEstimate(flops=1_000_000, bytes_accessed=1_000, transcendentals=0)
ORDER = (0, 2, 4, 6, 1, 3, 5, 7)
GATHERED = (0, 4, 2, 6, 1, 5, 3, 7)


def params(size=VMEM_BYTES):
    return pltpu.CompilerParams(vmem_limit_bytes=size)


def full_spec(shape):
    return pl.BlockSpec(shape, lambda *_: (0,) * len(shape))


def nt_dot(a, b):
    return lax.dot_general(a, b, (((1,), (1,)), ((), ())), preferred_element_type=F32)


def slots_kernel(units, scalar_ref, *refs):
    metas, (pick_ref, place_ref, gain_ref) = refs[:-3], refs[-3:]
    metas = [m.at[n] for m in metas for n in range(m.shape[0])]
    rows = max(units, 8)
    topk = metas[0].shape[0]
    tokens = metas[0].shape[1] // 4
    first = scalar_ref[0]
    expert = (lax.broadcasted_iota(jnp.int32, (rows, tokens), 0) + first).astype(F32)
    token = lax.broadcasted_iota(jnp.int32, (rows, tokens), 1)
    slot = lax.broadcasted_iota(jnp.int32, (units, SLOT, tokens), 1).astype(F32)
    before = (
        lax.broadcasted_iota(jnp.int32, (tokens, tokens), 0)
        < lax.broadcasted_iota(jnp.int32, (tokens, tokens), 1)
    ).astype(BF16)
    for r in range(GROUP):
        live = token < scalar_ref[1 + r]
        meta = metas[r][...].astype(F32)
        ids = meta[:, :tokens]
        weights = meta[:, tokens : 2 * tokens] + meta[:, 2 * tokens : 3 * tokens] + meta[:, 3 * tokens :]
        hit = jnp.zeros((rows, tokens), F32)
        gain = jnp.zeros((rows, tokens), F32)
        for k in range(topk):
            same = jnp.broadcast_to(ids[k : k + 1], (rows, tokens)) == expert
            hit = hit + jnp.where(same, 1.0, 0.0)
            gain = gain + jnp.where(same, jnp.broadcast_to(weights[k : k + 1], (rows, tokens)), 0.0)
        hit = jnp.where(live, hit, 0.0)
        position = jnp.dot(hit.astype(BF16), before, preferred_element_type=F32)
        position = jnp.where(hit > 0.5, position, -1.0)[:units]
        pick = jnp.where(jnp.broadcast_to(position[:, None, :], slot.shape) == slot, 1.0, 0.0)
        gains = jnp.sum(pick * gain[:units][:, None, :], axis=2, keepdims=True)
        gain_ref[:, r * SLOT : (r + 1) * SLOT, :] = jnp.broadcast_to(gains, (units, SLOT, 128))
        pick = pick.reshape(units * SLOT, tokens)
        pick_ref[r] = pick.astype(BF16)
        place_ref[r] = pick.T.astype(BF16)


def make_slots(metas, specs, tokens, scalars, units):
    slots = units * SLOT
    return pl.pallas_call(
        functools.partial(slots_kernel, units),
        grid_spec=pltpu.PrefetchScalarGridSpec(
            num_scalar_prefetch=1,
            grid=(1,),
            in_specs=specs,
            out_specs=[
                full_spec((GROUP, slots, tokens)),
                full_spec((GROUP, tokens, slots)),
                full_spec((units, GROUP * SLOT, 128)),
            ],
        ),
        out_shape=[
            jax.ShapeDtypeStruct((GROUP, slots, tokens), BF16),
            jax.ShapeDtypeStruct((GROUP, tokens, slots), BF16),
            jax.ShapeDtypeStruct((units, GROUP * SLOT, 128), F32),
        ],
        compiler_params=params(),
        cost_estimate=COST,
    )(scalars, *metas)


def expand_kernel(units, quarters, first, layout, final, scalar_ref, *refs):
    count = len(layout)
    groups, refs = refs[: quarters * count], refs[quarters * count :]
    if final:
        pick_ref, gate_hbm, up_hbm, start_ref, low_ref, table_ref = refs[:6]
        out_ref, gathered, both_ref, done, low_rows, tables = refs[6:]
    else:
        pick_ref, gate_hbm, up_hbm, out_ref, gathered, both_ref, done = refs
    tokens, wide = pick_ref.shape[2], gathered.shape[3]
    places = [slice(r * SLOT, (r + 1) * SLOT) for r in range(GROUP)]
    at = [
        pl.ds(pl.multiple_of((scalar_ref[0] ^ (first + turn)) * wide, wide), wide)
        for turn in range(quarters)
    ]

    block = min(units, 4)
    copies = []
    for g in range(units // block):
        part = pl.ds(g * block, block)
        for turn in range(quarters):
            for n, weight in enumerate((gate_hbm, up_hbm)):
                copy = pltpu.make_async_copy(
                    weight.at[part, at[turn], :], both_ref.at[turn, n, part], done.at[g, turn, n]
                )
                copy.start()
                copies.append(copy)

    def scatter(target, r, rows):
        target[:, places[r], :] = rows.astype(BF16).reshape(units, SLOT, rows.shape[1])

    for turn in range(quarters):
        for source, spots in zip(groups[turn * count : (turn + 1) * count], layout, strict=True):
            for n, r in enumerate(spots):
                if len(source.shape) == 2:
                    block_rows = source[:, at[turn]]
                elif source.shape[2] == wide:
                    block_rows = source[n, :tokens, :]
                else:
                    block_rows = source[n, :, at[turn]]
                scatter(gathered.at[turn], r, jnp.dot(pick_ref[r], block_rows, preferred_element_type=F32))
    if final:
        zero = jnp.zeros((SLOT, tokens), BF16)
        for r in range(GROUP):
            spread = jnp.concatenate([zero] * r + [low_ref[r]] + [zero] * (GROUP - 1 - r), axis=0)
            scatter(low_rows, r, nt_dot(pick_ref[r], spread))
            tables[places[r], :] = table_ref[scalar_ref[1 + r]]

    def one(unit, carry):
        value = None
        for turn in range(quarters):
            both = jnp.concatenate([both_ref[turn, 0, unit], both_ref[turn, 1, unit]], axis=1)
            product = jnp.dot(gathered[turn, unit], both, preferred_element_type=F32)
            value = product if value is None else value + product
        if final:
            value = value + jnp.dot(low_rows[unit], tables[...], preferred_element_type=F32)
            value = value + start_ref[unit]
            half = value.shape[1] // 2
            gate, up = value[:, :half], value[:, half:]
            out_ref[unit] = (gate / (1.0 + jnp.exp(-gate)) * up).astype(BF16)
        else:
            out_ref[unit] = value
        return carry

    for g in range(units // block):
        for copy in copies[g * 2 * quarters : (g + 1) * 2 * quarters]:
            copy.wait()
        lax.fori_loop(g * block, (g + 1) * block, one, 0, unroll=block)


def expand(sources, layout, first, scalars, pick, gate_weight, up_weight, final=None):
    units, width, share = gate_weight.shape
    wide = width // 4
    quarters = len(sources) // len(layout)
    rows = GROUP * SLOT
    args = list(sources) + [pick, gate_weight, up_weight]
    scratch = [
        pltpu.VMEM((quarters, units, rows, wide), BF16),
        pltpu.VMEM((quarters, 2, units, wide, share), BF16),
        pltpu.SemaphoreType.DMA((units, quarters, 2)),
    ]
    if final is None:
        out_shape = jax.ShapeDtypeStruct((units, rows, 2 * share), F32)
    else:
        args += list(final)
        out_shape = jax.ShapeDtypeStruct((units, rows, share), BF16)
        scratch += [pltpu.VMEM((units, rows, rows), BF16), pltpu.VMEM((rows, 2 * share), BF16)]
    count = len(sources) + 1
    vmem = pl.BlockSpec(memory_space=pltpu.VMEM)
    hbm = pl.BlockSpec(memory_space=pl.ANY)
    return pl.pallas_call(
        functools.partial(expand_kernel, units, quarters, first, layout, final is not None),
        in_specs=[pl.BlockSpec(memory_space=pltpu.SMEM)] + [vmem] * count + [hbm, hbm] + [vmem] * (len(args) - count - 2),
        out_specs=vmem,
        scratch_shapes=scratch,
        out_shape=out_shape,
        compiler_params=params(EXPAND_BYTES),
        cost_estimate=COST,
    )(scalars, *args)


def contract_kernel(units, jobs, parts, scalar_ref, down_hbm, hidden_ref, place_ref, gain_ref, *refs):
    outs, (table, down_ref, done) = refs[:-3], refs[-3:]
    wide = table.shape[2]
    copies = []
    for n, (part, q) in enumerate(jobs):
        at = pl.ds(pl.multiple_of(((scalar_ref[0] ^ q) * parts + part) * wide, wide), wide)
        copies.append(pltpu.make_async_copy(down_hbm.at[:, at, :], down_ref.at[n], done.at[n]))
        copies[n].start()
    for n in range(len(jobs)):
        copies[n].wait()

        def one(unit, carry, n=n):
            rows = nt_dot(hidden_ref[unit], down_ref[n, unit])
            gain = jnp.concatenate([gain_ref[unit]] * (wide // 128), axis=1)
            spot = pl.ds(pl.multiple_of(unit * SLOT, SLOT), SLOT)
            table[:, spot, :] = (rows * gain).astype(BF16).reshape(GROUP, SLOT, wide)
            return carry

        lax.fori_loop(0, units, one, 0, unroll=min(units, UNROLL))
        for r in range(GROUP):
            sums = jnp.dot(place_ref[r], table[r], preferred_element_type=F32)
            outs[n][r] = sums.astype(outs[n].dtype)


def contract(hidden, down_weight, place, gain, scalars, jobs, parts):
    units, width, share = down_weight.shape
    tokens = place.shape[1]
    wide = width // 4 // parts
    vmem = pl.BlockSpec(memory_space=pltpu.VMEM)
    return pl.pallas_call(
        functools.partial(contract_kernel, units, jobs, parts),
        in_specs=[pl.BlockSpec(memory_space=pltpu.SMEM), pl.BlockSpec(memory_space=pl.ANY)] + [vmem] * 3,
        out_specs=[vmem] * len(jobs),
        scratch_shapes=[
            pltpu.VMEM((GROUP, units * SLOT, wide), BF16),
            pltpu.VMEM((len(jobs), units, wide, share), BF16),
            pltpu.SemaphoreType.DMA((len(jobs),)),
        ],
        out_shape=[jax.ShapeDtypeStruct((GROUP, tokens, wide), BF16 if q % 2 else F32) for _, q in jobs],
        compiler_params=params(EXPAND_BYTES),
        cost_estimate=COST,
    )(scalars, down_weight, hidden, place, gain)


def xor_move(value, axis, bits):
    size = lax.axis_size(axis)
    return lax.ppermute(value, axis, [(i, i ^ bits) for i in range(size)])


def select_adapters(request_adapter, rows_local, row_index):
    wanted = request_adapter[:, None] * DOUBLE_RANK + jnp.arange(DOUBLE_RANK)[None, :]
    held = row_index * rows_local + jnp.arange(rows_local)
    return (wanted.reshape(-1)[:, None] == held[None, :]).astype(BF16)


def widen_tables(tables):
    is_gate = (jnp.arange(DOUBLE_RANK) < ADAPTER_RANK)[None, :, None]
    zero = jnp.zeros_like(tables)
    return jnp.concatenate([jnp.where(is_gate, tables, zero), jnp.where(is_gate, zero, tables)], axis=2)


def meta_of(token_experts, router_weight):
    left = router_weight.T
    terms = []
    for _ in range(3):
        term = lax.reduce_precision(left, 8, 7)
        terms.append(term.astype(BF16))
        left = left - term
    return jnp.concatenate([token_experts.T.astype(BF16)] + terms, axis=1)


def end_along_z(here):
    last = here[0]
    for k in (1, 2, 3):
        last = last + xor_move(here[k].astype(BF16), "dp", 2 * k).astype(F32)
    return last.astype(BF16)


def near_device(
    tokens,
    lengths,
    request_adapter,
    token_experts,
    router_weight,
    gate_weight,
    up_weight,
    down_weight,
    adapter_input_maps,
    adapter_output_maps,
):
    width = tokens.shape[1]
    units = gate_weight.shape[0]
    dp_count = lax.axis_size("dp")
    tp_count = lax.axis_size("tensor")
    i = lax.axis_index("dp")
    j = lax.axis_index("tensor")
    experts_all = units * dp_count // 2
    quarter = width // tp_count
    rel = i ^ jnp.array(ORDER, jnp.int32)
    tok_rows = tokens.shape[0]
    own = lax.dynamic_slice_in_dim(tokens, j * quarter, quarter, 1)

    block = jnp.concatenate([own, meta_of(token_experts, router_weight)], axis=0)
    ahead = [xor_move(block, "dp", n) for n in (1, 2, 4, 6)]
    layout = ((0,), (4, 1, 2, 3), (5, 6, 7))

    chosen = select_adapters(request_adapter, adapter_input_maps.shape[1], i)
    columns = nt_dot(chosen, adapter_input_maps)
    columns = columns.astype(BF16)

    halves = adapter_output_maps.reshape(adapter_output_maps.shape[0], -1)
    tables = jnp.dot(chosen, halves, preferred_element_type=F32).astype(BF16)
    share = halves.shape[1] // 2
    upper = i >= dp_count // 2
    first_expert = (i * units) % experts_all
    is_rel = rel[:, None] == jnp.arange(dp_count)[None, :]
    lengths_rel = jnp.sum(jnp.where(is_rel, lengths[None, :], 0), axis=1)
    slot_scalars = jnp.concatenate([first_expert[None], lengths_rel]).astype(jnp.int32)
    scalars = jnp.concatenate([j[None], rel]).astype(jnp.int32)
    strips = quarter // share

    def strip(rows):
        return [rows[:, n * share : (n + 1) * share] for n in range(rows.shape[1] // share)]

    def halve(columns, given, bits):
        kept = columns.shape[0] // 2
        pairs = columns.reshape((-1, 2, DOUBLE_RANK, quarter))
        side = (i // bits) % 2
        mine_half = lax.dynamic_index_in_dim(pairs, side, 1, keepdims=False).reshape(kept, quarter)
        sent_half = lax.dynamic_index_in_dim(pairs, 1 - side, 1, keepdims=False).reshape(kept, quarter)
        got = xor_move(jnp.concatenate(strip(sent_half) + given, axis=0), "dp", bits)
        more = jnp.concatenate([got[n * kept : (n + 1) * kept] for n in range(strips)], axis=1)
        got = got[strips * kept :]
        size = given[0].shape[0]
        return mine_half + more, [got[n * size : (n + 1) * size] for n in range(len(given))]

    tables = strip(tables)
    columns, came = halve(columns, tables, 1)
    tables = [t + c for t, c in zip(tables, came, strict=True)]

    ahead, columns, tables = lax.optimization_barrier((ahead, columns, tables))
    behind = xor_move(jnp.stack(ahead[1:]), "dp", 1)
    ahead = jnp.stack(ahead)
    side_ahead = xor_move(ahead, "tensor", 2)
    core_ahead = xor_move(ahead, "tensor", 1)
    columns, came = halve(columns, tables, 2)
    tables = [t + c for t, c in zip(tables, came, strict=True)]
    mine, other = jnp.where(upper, tables[1], tables[0]), jnp.where(upper, tables[0], tables[1])
    columns, came = halve(columns, [other], 4)
    tables = mine + came[0]
    low = nt_dot(columns, own)
    low = low + xor_move(low, "tensor", 1)

    behind, low, tables, side_ahead = lax.optimization_barrier((behind, low, tables, side_ahead))
    low = low + xor_move(low, "tensor", 2)
    side_behind = xor_move(behind, "tensor", 2)
    core_behind = xor_move(behind, "tensor", 1)
    low = low.astype(BF16)[None]
    for bits in (4, 2):
        low = jnp.concatenate([low, xor_move(low, "dp", bits)], axis=0)
    both_ahead = xor_move(side_ahead, "tensor", 1)
    tables = widen_tables(tables.reshape(dp_count, DOUBLE_RANK, share))

    routes = block.shape[0] - tok_rows
    meta_specs = [
        pl.BlockSpec((n, routes, quarter), lambda *_: (0, tok_rows // routes, 0)) for n in (1, 3, 1, 3)
    ]
    meta_specs[2] = pl.BlockSpec((1, routes, quarter), lambda *_: (0, tok_rows // routes, 0))
    meta_specs[1] = pl.BlockSpec((3, routes, quarter), lambda *_: (0, tok_rows // routes, 0))
    pick, place, gain = make_slots(
        [block[None], ahead[1:], ahead[:1], behind], meta_specs, tok_rows, slot_scalars, units
    )

    def sources(*pairs):
        return [x for pair in pairs for x in (tokens,) + pair]

    start = expand(
        sources((ahead, behind), (core_ahead, core_behind)), layout, 0, scalars, pick, gate_weight, up_weight
    )
    start, side_behind, low = lax.optimization_barrier((start, side_behind, low))
    low = jnp.concatenate([low, xor_move(low, "dp", 1)], axis=0)
    low = jnp.stack([low[GATHERED.index(n)] for n in ORDER])
    both_behind = xor_move(side_behind, "tensor", 1)
    hidden = expand(
        sources((side_ahead, side_behind), (both_ahead, both_behind)),
        layout,
        2,
        scalars,
        pick,
        gate_weight,
        up_weight,
        (start, low, tables),
    )

    def core_sum(send, keep):
        return keep + xor_move(send, "tensor", 1).astype(F32)

    early = contract(hidden, down_weight, place, gain, scalars, ((1, 3), (1, 2), (0, 3), (0, 2)), 2)
    there = core_sum(*early[2:]).astype(BF16)
    second_there = core_sum(*early[:2])
    there, second_there, hidden = lax.optimization_barrier((there, second_there, hidden))
    above = xor_move(there[4:], "tensor", 2)
    below = xor_move(there[:4], "tensor", 2)
    across = xor_move(second_there[4:].astype(BF16), "dp", 1)

    late = contract(hidden, down_weight, place, gain, scalars, ((0, 1), (0, 0), (1, 1), (1, 0)), 2)
    late, above, across = lax.optimization_barrier((late, above, across))
    second_there = xor_move((second_there[:4] + across.astype(F32)).astype(BF16), "tensor", 2)
    here = core_sum(*late[:2])
    given = (here[4:] + above.astype(F32)).astype(BF16)
    here = here[:4] + below.astype(F32) + xor_move(given, "dp", 1).astype(F32)
    first = end_along_z(here)
    here = core_sum(*late[2:])
    here = here[:4] + xor_move(here[4:].astype(BF16), "dp", 1).astype(F32) + second_there.astype(F32)
    second = end_along_z(here)
    return jnp.concatenate([first, second], axis=1)


def any_device(
    tokens,
    lengths,
    request_adapter,
    token_experts,
    router_weight,
    gate_weight,
    up_weight,
    down_weight,
    adapter_input_maps,
    adapter_output_maps,
):
    tok_rows, width = tokens.shape
    units = gate_weight.shape[0]
    dp_count = lax.axis_size("dp")
    tp_count = lax.axis_size("tensor")
    i = lax.axis_index("dp")
    j = lax.axis_index("tensor")
    experts_all = units * dp_count // 2
    quarter = width // tp_count
    meta = lax.all_gather(meta_of(token_experts, router_weight), "dp", axis=0)
    rows = lax.all_gather(tokens, "dp", axis=0)
    maps = lax.all_gather(adapter_input_maps, "dp", axis=1, tiled=True)
    adapter = jnp.sum(jnp.where(jnp.arange(dp_count) == i, request_adapter, 0))
    columns = nt_dot(select_adapters(adapter[None], maps.shape[1], 0), maps).astype(BF16)
    x_part = lax.dynamic_slice_in_dim(tokens, j * quarter, quarter, 1)
    low = lax.psum(nt_dot(columns, x_part), "tensor").astype(BF16)
    low = lax.all_gather(low, "dp", axis=0)
    every = lax.all_gather(adapter_output_maps, "dp", axis=0, tiled=True)
    half = jnp.where(i * units >= experts_all, every[:, 1], every[:, 0])
    tables = jnp.dot(
        select_adapters(request_adapter, half.shape[0], 0), half, preferred_element_type=F32
    ).astype(BF16)
    tables = widen_tables(tables.reshape(dp_count, DOUBLE_RANK, half.shape[1]))
    first_expert = (i * units) % experts_all
    natural = jnp.concatenate([j[None], jnp.arange(GROUP)]).astype(jnp.int32)

    def one_group(group):
        meta_g, rows_g, low_g, tables_g, lengths_g = group
        pick, place, gain = make_slots(
            [meta_g],
            [full_spec(meta_g.shape)],
            tok_rows,
            jnp.concatenate([first_expert[None], lengths_g]).astype(jnp.int32),
            units,
        )
        layout = (tuple(range(GROUP)),)

        start = expand([rows_g] * 2, layout, 0, natural, pick, gate_weight, up_weight)
        hidden = expand(
            [rows_g] * 2, layout, 2, natural, pick, gate_weight, up_weight, (start, low_g, tables_g)
        )
        jobs = tuple((0, q) for q in range(4))
        sums = contract(hidden, down_weight, place, gain, natural, jobs, 1)
        return tuple(a.astype(BF16) for a in sums)

    groups = dp_count // GROUP
    grouped = [
        a.reshape((groups, GROUP) + a.shape[1:]) for a in (meta, rows, low, tables, lengths)
    ]
    sums = lax.map(one_group, tuple(grouped))
    sums = [a.reshape(dp_count * tok_rows, quarter) for a in sums]
    here = sums[0].astype(F32)
    for q in range(1, 4):
        here = here + xor_move(sums[q], "tensor", q).astype(F32)
    return lax.psum_scatter(here, "dp", scatter_dimension=0, tiled=True).astype(BF16)


def solution(mesh):
    near = mesh.shape["dp"] == 8 and mesh.shape["tensor"] == 4
    in_specs = (
        P("dp", None),
        P(),
        P(),
        P("dp", None),
        P("dp", None),
        P("dp", None, "tensor"),
        P("dp", None, "tensor"),
        P("dp", None, "tensor"),
        P("tensor", "dp"),
        P("dp", None, "tensor"),
    )
    return jax.shard_map(
        near_device if near else any_device,
        mesh=mesh,
        in_specs=in_specs,
        out_specs=P("dp", "tensor"),
        check_vma=False,
    )
```
